32 devices in a mesh: dp: 4 (over y, x), expert: 8 (over z, core).
Axes of the slice: x: 2, y: 2, z: 4, core: 2. Of those that a mesh axis runs over, the one named last changes fastest.
Arguments:
- tokens: bfloat16 [4096, 768], P(('dp', 'expert')), may hold values from -6 to 6
- cotangent: bfloat16 [4096, 768], P(('dp', 'expert')), may hold values from -6 to 6
- doc_lengths: int32 [32, 4], P(('dp', 'expert')), may hold values from 1 to 96, 128 in all within a row
- routes: int32 [4096, 2], P(('dp', 'expert')), may hold values from 0 to 7, all different within a row; in each aligned block of 128 rows (0 to 127, 128 to 255, ...) at most 33 rows name the same one
- rel_bucket: int32 [96], replicated, may hold values from 0 to 31
- norm1: bfloat16 [768], P(('dp', 'expert')), may hold values from 0.099609375 to 1.8984375
- attn_in: bfloat16 [768, 2304], P(('dp', 'expert')), may hold values from -1.5 to 1.5
- attn_out: bfloat16 [768, 768], P(None, ('dp', 'expert')), may hold values from -0.625 to 0.625
- bias_table: float32 [32, 12], replicated, may hold values from -4 to 4
- norm2: bfloat16 [768], P(('dp', 'expert')), may hold values from 0.099609375 to 1.8984375
- router: bfloat16 [768, 8], P(('dp', 'expert')), may hold values from -5 to 5
- w_gate_up: bfloat16 [8, 768, 2, 3072], P('expert', None, None, 'dp'), may hold values from -0.21875 to 0.21875
- w_down: bfloat16 [8, 3072, 768], P('expert', 'dp'), may hold values from -0.109375 to 0.109375
Outputs:
- output: bfloat16 [4096, 768], P(('dp', 'expert'))
- d_tokens: float32 [4096, 768], P(('dp', 'expert'))
- d_norm1: float32 [768], P(('dp', 'expert'))
- d_attn_in: float32 [768, 2304], P(('dp', 'expert'))
- d_attn_out: float32 [768, 768], P(None, ('dp', 'expert'))
- d_bias_table: float32 [32, 12], replicated
- d_norm2: float32 [768], P(('dp', 'expert'))
- d_router: float32 [768, 8], P(('dp', 'expert'))
- d_w_gate_up: float32 [8, 768, 2, 3072], P('expert', None, None, 'dp')
- d_w_down: float32 [8, 3072, 768], P('expert', 'dp')
The draws below stay inside these ranges and needn't reach their ends.
Inputs may be any that keep to these rules, and one draw needn't show every extreme that they name: `routes`: each row names 2 different experts; within the 128 rows of one pack no expert is named more than 33 times, a bound that some block reaches. `doc_lengths`: each row holds 4 lengths that sum to 128, the largest exactly 96.
All inputs are finite; a program needn't handle non-finite values.
Results may differ from the reference program's by a relative error of at most 0.012.
The reference program's roundings to bfloat16 on the way count: a program that leaves them out, or rounds other values in their place, can miss the bound.
Values may be sent and summed in bfloat16 or wider, within the bound.
No kernel may reach another device: no remote copies, remote signals or barrier semaphores. Data moves between devices by JAX's collectives and lax.ppermute only.
A program may use at most 192 MiB of HBM per device.

```python
import math
import jax
import jax.numpy as jnp
import numpy as np
from jax import lax

D = 768
H = 12
HD = 64
FF = 3072
TOP = 2
NB = 32
LMAX = 96
TOK_DEV = 128
DOCS = 4
EXPERTS = 8
CAP = 33
PACKS = 32
TOKENS = 4096


def draw_attn_in(key, part):
    first_key = jax.random.fold_in(key, 0)
    entries = jnp.clip(jax.random.normal(first_key, (D, 3 * D), jnp.float32), -6.0, 6.0)
    return (entries * D ** (-0.5)).astype(jnp.bfloat16)


def draw_router(key, part):
    first_key = jax.random.fold_in(key, 0)
    entries = 2.0 * jnp.clip(jax.random.normal(first_key, (D, EXPERTS), jnp.float32), -6.0, 6.0)
    return (entries * D ** (-0.5)).astype(jnp.bfloat16)


def with_ends(values, stream_key, smallest, largest):
    shape = values.shape
    place = [jax.random.randint(jax.random.fold_in(stream_key, axis), (), 0, shape[axis]) for axis in range(len(shape))]
    values = values.at[tuple(place)].set(smallest)
    longest = shape.index(max(shape))
    place[longest] = (place[longest] + 1) % shape[longest]
    return values.at[tuple(place)].set(largest)


def strengthened(values, rng, source, target, parts, factor):
    owner, partner = [(jnp.arange(values.shape[axis_at]) // (values.shape[axis_at] // parts)).reshape([-1 if axis == axis_at else 1 for axis in range(values.ndim)]) for axis_at in (source, target)]
    chosen = jax.random.permutation(rng, parts)[partner]
    strong = (owner == chosen) | (owner == (partner + parts // 2) % parts)
    return jnp.where(strong, factor * values, values)


def block_levels(key, dims, cuts, least, high):
    def one(axis_at, shards_of):
        draws = jax.random.uniform(jax.random.fold_in(jax.random.fold_in(key, 6), axis_at), (shards_of,), jnp.float32, least / len(cuts), high / len(cuts))
        return jnp.repeat(jnp.exp(draws), dims[axis_at] // shards_of).reshape((-1,) + (1,) * (len(dims) - axis_at - 1))

    factor_of = one(*cuts[0])
    for cut in cuts[1:]:
        factor_of = factor_of * one(*cut)
    return factor_of


def split_up(count, total, most, slope):
    portions = [(1 << 20) // math.isqrt(grade ** slope) + 1 for grade in range(2, count + 1)]
    spare, counts = total - most - (count - 1), [1] * (count - 1)
    while spare > 0:
        free = [i for i in range(count - 1) if counts[i] < most]
        mass, left = sum([portions[i] for i in free]), spare
        for i in free:
            addition = min(most - counts[i], max(1, left * portions[i] // mass), spare)
            counts[i] = counts[i] + addition
            spare = spare - addition
    return np.array([most] + counts)


def ragged_sizes(stream_key, number_of, total, most, skew):
    if number_of == 2:
        one = jax.random.randint(stream_key, (), max(1, total - most), min(most, total - 1) + 1)
        return jnp.stack([one, total - one])
    tallies = jnp.asarray(split_up(number_of, total, most, skew), jnp.int32)
    pairs = (number_of - 1) // 2
    donor, sink = tallies[1:1 + 2 * pairs:2], tallies[2:2 + 2 * pairs:2]
    slack = jnp.minimum(donor - 1, most - sink)
    moved = jax.random.randint(jax.random.fold_in(stream_key, 1), (pairs,), 0, 1 << 20) % (slack + 1)
    tallies = tallies.at[1:1 + 2 * pairs:2].set(donor - moved).at[2:2 + 2 * pairs:2].set(sink + moved)
    return tallies[jax.random.permutation(jax.random.fold_in(stream_key, 2), number_of)]


def routed_block(rng, own, number, rows, number_of, top, most, slope):
    sequence = jax.random.permutation(rng, number_of)
    crowded, usual = load_shares(number_of, rows * top, most, slope, True), load_shares(number_of, rows * top, most, slope, False)
    places = jnp.arange(number_of)

    def named(tallies, offset_by):
        used = int((tallies > 0).sum())
        fixed = max(1, used // 4)
        passed = fixed + (places - fixed + offset_by * (used - fixed)) % max(1, number_of - fixed)
        return jnp.zeros((number_of,), jnp.int32).at[sequence[jnp.where(places < fixed, places, passed)]].set(jnp.asarray(tallies, jnp.int32))

    tallies = jnp.where(number % 4 == 0, named(crowded, number // 4), named(usual, number - number // 4 - 1))
    mixed = jax.random.permutation(jax.random.fold_in(own, 3), number_of)
    giver, sink = mixed[0:number_of // 2 * 2:2], mixed[1:number_of // 2 * 2:2]
    slack = jnp.minimum(tallies[giver] - 1, most - tallies[sink]) // 2
    slack = jnp.where((giver == sequence[0]) | (sink == sequence[0]) | (tallies[sink] == 0), 0, jnp.maximum(slack, 0))
    passed = jax.random.randint(jax.random.fold_in(own, 4), (number_of // 2,), 0, 1 << 20) % (slack + 1)
    tallies = tallies.at[giver].add(-passed).at[sink].add(passed)
    items = jnp.searchsorted(jnp.cumsum(tallies), jnp.arange(rows * top), side="right").astype(jnp.int32)
    table = items.reshape(top, rows).T
    table = table[jax.random.permutation(jax.random.fold_in(own, 1), rows)]
    offset_by = jax.random.randint(jax.random.fold_in(own, 2), (rows, 1), 0, top)
    return jnp.take_along_axis(table, (jnp.arange(top)[None, :] + offset_by) % top, axis=1)


def load_shares(number_of, total, reach, lean, full):
    loads = [(1 << 20) // math.isqrt(grade ** lean) + 1 for grade in range(1, number_of + 1)]
    largest = reach if full else min(reach, max(-(-total // number_of), total * loads[0] // sum(loads)))
    least = 1 if total - largest >= number_of - 1 else 0
    counts, rest = [largest] + [least] * (number_of - 1), total - largest - least * (number_of - 1)
    while rest > 0:
        candidates = [i for i in range(1, number_of) if counts[i] < largest] or [i for i in range(1, number_of) if counts[i] < reach]
        whole, remaining = sum([loads[i] for i in candidates]), rest
        for i in candidates:
            extra = min(reach - counts[i], max(1, remaining * loads[i] // whole), rest)
            counts[i] = counts[i] + extra
            rest = rest - extra
    return np.array(counts)


def scatter_about(stream_key, shape, scale, limit, cuts=(), held_as=jnp.bfloat16):
    gain = block_levels(stream_key, shape, cuts, -0.22, 0.18) if cuts else 1.0
    drawn = jax.random.normal(stream_key, shape, jnp.float32) * scale * gain
    return jnp.minimum(jnp.maximum(drawn, -limit), limit).astype(held_as)


def noise_with(rng, shape, spread, most, cuts, heavy, kind=jnp.bfloat16):
    drawn = spread * jax.random.normal(rng, shape, jnp.float32)
    if cuts:
        drawn = drawn * block_levels(rng, shape, cuts, -0.22, 0.18)
    return jnp.clip(strengthened(drawn, jax.random.fold_in(rng, 3), *heavy), -most, most).astype(kind)


def setup_inputs(seed: int = 0) -> dict:
    streams_of = jax.random.split(jax.random.key(seed), 14)
    tokens = scatter_about(streams_of[0], (TOKENS, D), 1.0, 6.0, ((0, 32),))
    cotangent = noise_with(streams_of[1], (TOKENS, D), 1.0, 6.0, ((0, 32),), (0, 1, 32, 2.75))
    doc_lengths = jax.vmap(lambda own: ragged_sizes(own, DOCS, TOK_DEV, LMAX, 2))(jax.random.split(streams_of[2], PACKS)).reshape((PACKS, DOCS)).astype(jnp.int32)
    routes_keys = jax.random.split(jax.random.fold_in(streams_of[3], 1), TOKENS // TOK_DEV)
    routes_turns = jax.random.permutation(jax.random.fold_in(streams_of[3], 3), TOKENS // TOK_DEV)
    routes = jax.vmap(lambda own, number: routed_block(jax.random.fold_in(streams_of[3], 2), own, number, TOK_DEV, EXPERTS, TOP, CAP, 2))(routes_keys, routes_turns).reshape((TOKENS, TOP))
    rel_bucket = with_ends(jax.random.randint(streams_of[4], (LMAX,), 0, NB), jax.random.fold_in(streams_of[4], 1), 0, NB - 1).astype(jnp.int32)
    norm1 = jnp.clip(1.0 + 0.18 * jax.random.normal(streams_of[5], (D,), jnp.float32), 0.099609375, 1.8984375).astype(jnp.bfloat16)
    attn_in = draw_attn_in(jax.random.fold_in(streams_of[13], 71), 0)
    attn_out = scatter_about(streams_of[7], (D, D), (D // 8) ** -0.5, 0.625, ((1, 32),))
    bias_table = scatter_about(streams_of[8], (NB, H), 1.0, 4.0, (), jnp.float32)
    norm2 = jnp.clip(1.0 + 0.18 * jax.random.normal(streams_of[9], (D,), jnp.float32), 0.099609375, 1.8984375).astype(jnp.bfloat16)
    router = draw_router(jax.random.fold_in(streams_of[13], 71), 0)
    w_gate_up = scatter_about(streams_of[11], (EXPERTS, D, 2, FF), D ** -0.5, 0.21875, ((0, 8), (3, 4)))
    w_down = scatter_about(streams_of[12], (EXPERTS, FF, D), FF ** -0.5, 0.109375, ((0, 8), (1, 4)))
    return dict(tokens=tokens, cotangent=cotangent, doc_lengths=doc_lengths, routes=routes, rel_bucket=rel_bucket, norm1=norm1, attn_in=attn_in, attn_out=attn_out, bias_table=bias_table, norm2=norm2, router=router, w_gate_up=w_gate_up, w_down=w_down)


EPSILON = 1e-06
GELU_COEF = 0.7978845608028654
GELU_CUBE = 0.044715
SCORE_SCALE = 0.125

def rounded(array):
    return lax.optimization_barrier(array.astype(jnp.bfloat16)).astype(jnp.float32)

def gelu_parts(gate_in):
    inner_arg = GELU_COEF * (gate_in + GELU_CUBE * gate_in * gate_in * gate_in)
    tanh_part = jnp.tanh(inner_arg)
    result = 0.5 * gate_in * (1.0 + tanh_part)
    derivative = 0.5 * (1.0 + tanh_part) + 0.5 * gate_in * (1.0 - tanh_part * tanh_part) * GELU_COEF * (1.0 + 3.0 * GELU_CUBE * gate_in * gate_in)
    return (result, derivative)

def rms_forward(values, gain_vec):
    inverse = lax.rsqrt(lax.optimization_barrier(jnp.mean(values * values, axis=-1, keepdims=True)) + EPSILON)
    return (inverse, values * inverse * gain_vec.astype(jnp.float32))

def rms_backward(values, inverse, gain_vec, d_normed):
    scaled = gain_vec.astype(jnp.float32) * d_normed
    d_gain = lax.optimization_barrier(jnp.sum(d_normed * values * inverse, axis=0))
    d_values = inverse * scaled - values * (inverse * inverse * inverse) * lax.optimization_barrier(jnp.mean(scaled * values, axis=-1, keepdims=True))
    return (d_values, d_gain)

def pack_layout(lengths_row, rows_here):
    doc_ends = jnp.cumsum(lengths_row)
    places = jnp.arange(rows_here, dtype=jnp.int32)
    doc_index = lax.optimization_barrier(jnp.sum((places[:, None] >= doc_ends[None, :]).astype(jnp.int32), axis=1))
    allowed = (doc_index[:, None] == doc_index[None, :]) & (places[None, :] <= places[:, None])
    distance = jnp.clip(places[:, None] - places[None, :], 0, LMAX - 1).astype(jnp.int32)
    return (allowed, distance)

def pack_scores(qkv_rows, lengths_row, bias_dist):
    rows_here = qkv_rows.shape[0]
    allowed, distance = pack_layout(lengths_row, rows_here)
    pieces = qkv_rows.astype(jnp.float32).reshape(rows_here, 3, H, HD).transpose(1, 2, 0, 3)
    queries, head_keys, head_values = (pieces[0], pieces[1], pieces[2])
    bias_heads = jnp.transpose(bias_dist[distance], (2, 0, 1))
    scores = jnp.einsum('hid,hjd->hij', queries, head_keys) * SCORE_SCALE + bias_heads
    scores = jnp.where(allowed[None], scores, -jnp.inf)
    return (scores, allowed, distance, queries, head_keys, head_values)

def attend_forward(pack_item, bias_dist):
    qkv_rows, lengths_row = pack_item
    scores, allowed, distance, queries, head_keys, head_values = pack_scores(qkv_rows, lengths_row, bias_dist)
    row_top = lax.optimization_barrier(jnp.max(scores, axis=-1, keepdims=True))
    log_total = row_top + jnp.log(lax.optimization_barrier(jnp.sum(jnp.exp(scores - row_top), axis=-1, keepdims=True)))
    attn_weights = rounded(jnp.exp(scores - log_total))
    context = jnp.einsum('hij,hjd->ihd', attn_weights, head_values)
    context = context.reshape(qkv_rows.shape[0], H * HD).astype(jnp.bfloat16)
    return (context, log_total[:, :, 0])

def attend_backward(pack_item, bias_dist):
    qkv_rows, lengths_row, log_total, d_context = pack_item
    rows_here = qkv_rows.shape[0]
    scores, allowed, distance, queries, head_keys, head_values = pack_scores(qkv_rows, lengths_row, bias_dist)
    attn_probs = jnp.exp(scores - log_total[:, :, None])
    attn_weights = rounded(attn_probs)
    d_heads = d_context.astype(jnp.float32).reshape(rows_here, H, HD).transpose(1, 0, 2)
    d_probs = jnp.einsum('hid,hjd->hij', d_heads, head_values)
    row_delta = lax.optimization_barrier(jnp.sum(attn_probs * d_probs, axis=-1, keepdims=True))
    d_scores = jnp.where(allowed[None], attn_probs * (d_probs - row_delta), 0.0)
    d_scores_b = rounded(d_scores)
    d_queries = rounded(jnp.einsum('hij,hjd->hid', d_scores_b, head_keys) * SCORE_SCALE)
    d_keys = rounded(jnp.einsum('hij,hid->hjd', d_scores_b, queries) * SCORE_SCALE)
    d_values = rounded(jnp.einsum('hij,hid->hjd', attn_weights, d_heads))
    d_qkv = jnp.stack([d_queries, d_keys, d_values]).transpose(2, 0, 1, 3).reshape(rows_here, 3 * H * HD).astype(jnp.bfloat16)
    d_dist = jax.ops.segment_sum(d_scores.transpose(1, 2, 0).reshape(-1, H), distance.reshape(-1), num_segments=LMAX)
    return (d_qkv, d_dist)

def reference(tokens, cotangent, doc_lengths, routes, rel_bucket, norm1, attn_in, attn_out, bias_table, norm2, router, w_gate_up, w_down):
    pack_count = TOKENS // TOK_DEV
    inputs = tokens.astype(jnp.float32)
    inv_one, normed_one = rms_forward(inputs, norm1)
    normed_one = normed_one.astype(jnp.bfloat16)
    qkv_rows = jnp.dot(normed_one, attn_in, preferred_element_type=jnp.float32).astype(jnp.bfloat16)
    qkv_packs = qkv_rows.reshape(pack_count, TOK_DEV, 3 * D)
    bias_dist = bias_table[rel_bucket]

    def forward_pack(pack_item):
        return attend_forward(pack_item, bias_dist)
    context, log_total = lax.map(forward_pack, (qkv_packs, doc_lengths))
    context = context.reshape(TOKENS, D)
    residual = inputs + jnp.dot(context, attn_out, preferred_element_type=jnp.float32)
    inv_two, normed_two = rms_forward(residual, norm2)
    normed_two = normed_two.astype(jnp.bfloat16)
    logits = jnp.dot(normed_two, router, preferred_element_type=jnp.float32)
    route_picks = (routes[:, :, None] == jnp.arange(EXPERTS, dtype=jnp.int32)[None, None, :]).astype(jnp.float32)
    chosen_logits = lax.optimization_barrier(jnp.sum(route_picks * logits[:, None, :], axis=2))
    chosen_top = lax.optimization_barrier(jnp.max(chosen_logits, axis=1, keepdims=True))
    chosen_exp = jnp.exp(chosen_logits - chosen_top)
    route_weight = chosen_exp / lax.optimization_barrier(jnp.sum(chosen_exp, axis=1, keepdims=True))
    flat_routes = routes.reshape(pack_count, TOK_DEV * TOP)
    route_hits = (flat_routes[:, :, None] == jnp.arange(EXPERTS, dtype=jnp.int32)[None, None, :]).astype(jnp.int32)
    earlier = jnp.cumsum(route_hits, axis=1) - route_hits
    slot_index = lax.optimization_barrier(jnp.sum(earlier * route_hits, axis=2)).astype(jnp.int32)
    column = jnp.arange(pack_count, dtype=jnp.int32)[:, None] * CAP + slot_index
    route_ids = jnp.arange(TOKENS * TOP, dtype=jnp.int32).reshape(pack_count, TOK_DEV * TOP)
    slot_table = jnp.full((EXPERTS, pack_count * CAP), TOKENS * TOP, jnp.int32)
    slot_table = slot_table.at[flat_routes.reshape(-1), column.reshape(-1)].set(route_ids.reshape(-1))
    zero_row = jnp.zeros((1, D), jnp.bfloat16)
    route_rows = jnp.concatenate([jnp.repeat(normed_two, TOP, axis=0), zero_row], axis=0)
    d_expert_out = (route_weight[:, :, None] * cotangent.astype(jnp.float32)[:, None, :]).astype(jnp.bfloat16)
    d_route_in = jnp.concatenate([d_expert_out.reshape(TOKENS * TOP, D), zero_row], axis=0)

    def one_expert(expert_item):
        slot_rows, weight_up, weight_down = expert_item
        row_block = route_rows[slot_rows]
        d_block = d_route_in[slot_rows]
        up_flat = weight_up.reshape(D, 2 * FF)
        gate_up = jnp.dot(row_block, up_flat, preferred_element_type=jnp.float32).reshape(-1, 2, FF)
        activated, derivative = gelu_parts(gate_up[:, 0])
        hidden = (activated * gate_up[:, 1]).astype(jnp.bfloat16)
        produced = jnp.dot(hidden, weight_down, preferred_element_type=jnp.float32).astype(jnp.bfloat16)
        d_hidden = jnp.dot(d_block, weight_down.T, preferred_element_type=jnp.float32)
        d_weight_down = jnp.dot(hidden.T, d_block, preferred_element_type=jnp.float32)
        d_gate_up = jnp.stack([d_hidden * gate_up[:, 1] * derivative, d_hidden * activated], axis=1).astype(jnp.bfloat16)
        d_gate_flat = d_gate_up.reshape(-1, 2 * FF)
        d_weight_up = jnp.dot(row_block.T, d_gate_flat, preferred_element_type=jnp.float32).reshape(D, 2, FF)
        d_rows = jnp.dot(d_gate_flat, up_flat.T, preferred_element_type=jnp.float32).astype(jnp.bfloat16)
        return (produced, d_rows, d_weight_up, d_weight_down)
    produced, d_rows, d_w_gate_up, d_w_down = lax.map(one_expert, (slot_table, w_gate_up, w_down))
    flat_index = slot_table.reshape(-1)
    expert_out = jnp.zeros((TOKENS * TOP + 1, D), jnp.float32).at[flat_index].set(produced.reshape(-1, D).astype(jnp.float32))
    expert_out = expert_out[:-1].reshape(TOKENS, TOP, D)
    output = (residual + lax.optimization_barrier(jnp.sum(route_weight[:, :, None] * expert_out, axis=1))).astype(jnp.bfloat16)
    grad_out = cotangent.astype(jnp.float32)
    d_route_weight = lax.optimization_barrier(jnp.sum(grad_out[:, None, :] * expert_out, axis=2))
    route_delta = d_route_weight - lax.optimization_barrier(jnp.sum(d_route_weight * route_weight, axis=1, keepdims=True))
    d_logits = lax.optimization_barrier(jnp.sum(route_picks * (route_weight * route_delta)[:, :, None], axis=1)).astype(jnp.bfloat16)
    d_router = jnp.dot(normed_two.T, d_logits, preferred_element_type=jnp.float32)
    d_routes = jnp.zeros((TOKENS * TOP + 1, D), jnp.float32).at[flat_index].set(d_rows.reshape(-1, D).astype(jnp.float32))
    d_routes = d_routes[:-1].reshape(TOKENS, TOP, D)
    d_normed_two = lax.optimization_barrier(jnp.sum(d_routes, axis=1)) + jnp.dot(d_logits, router.T, preferred_element_type=jnp.float32)
    d_resid_part, d_norm2 = rms_backward(residual, inv_two, norm2, d_normed_two)
    d_residual = grad_out + d_resid_part
    d_residual_b = d_residual.astype(jnp.bfloat16)
    d_attn_out = jnp.dot(context.T, d_residual_b, preferred_element_type=jnp.float32)
    d_context = jnp.dot(d_residual_b, attn_out.T, preferred_element_type=jnp.float32).astype(jnp.bfloat16)

    def backward_pack(pack_item):
        return attend_backward(pack_item, bias_dist)
    d_qkv, d_dist = lax.map(backward_pack, (qkv_packs, doc_lengths, log_total, d_context.reshape(pack_count, TOK_DEV, D)))
    d_qkv = d_qkv.reshape(TOKENS, 3 * D)
    d_bias_table = jax.ops.segment_sum(lax.optimization_barrier(jnp.sum(d_dist, axis=0)), rel_bucket, num_segments=NB)
    d_attn_in = jnp.dot(normed_one.T, d_qkv, preferred_element_type=jnp.float32)
    d_normed_one = jnp.dot(d_qkv, attn_in.T, preferred_element_type=jnp.float32)
    d_input_part, d_norm1 = rms_backward(inputs, inv_one, norm1, d_normed_one)
    d_tokens = d_residual + d_input_part
    return (output, d_tokens, d_norm1, d_attn_in, d_attn_out, d_bias_table, d_norm2, d_router, d_w_gate_up, d_w_down)
```

```python
import jax
import jax.numpy as jnp
from jax import lax
from jax.sharding import PartitionSpec as P

D = 768
H = 12
HD = 64
TOP = 2
NB = 32
LMAX = 96

EPSILON = 1e-06
GELU_COEF = 0.7978845608028654
GELU_CUBE = 0.044715
SCORE_SCALE = 0.125

BF = jnp.bfloat16
F32 = jnp.float32


def gelu_parts(gate_in):
    inner_arg = GELU_COEF * (gate_in + GELU_CUBE * gate_in * gate_in * gate_in)
    tanh_part = jnp.tanh(inner_arg)
    result = 0.5 * gate_in * (1.0 + tanh_part)
    derivative = 0.5 * (1.0 + tanh_part) + 0.5 * gate_in * (
        1.0 - tanh_part * tanh_part
    ) * GELU_COEF * (1.0 + 3.0 * GELU_CUBE * gate_in * gate_in)
    return (result, derivative)


def mm(a, b, dims):
    return lax.dot_general(a, b, (dims, ((), ())), preferred_element_type=F32)


def dp_send(x, k):
    size = lax.axis_size("dp")
    return lax.ppermute(x, "dp", [(i, (i + k) % size) for i in range(size)])


def roll_blocks(blocks, me):
    n = len(blocks)
    twice = jnp.stack(blocks + blocks[:-1], axis=0)
    return lax.dynamic_slice_in_dim(twice, (n - me) % n, n, axis=0)


def unroll_blocks(stacked, me, axis=0):
    n = stacked.shape[axis]
    return [lax.dynamic_index_in_dim(stacked, (me + j) % n, axis, keepdims=False) for j in range(n)]


def direct(size):
    return size <= 8


def ex_pairs(size, shift, flip):
    ring = size // 2
    return [
        (2 * z + c, 2 * ((z + shift) % ring) + (c ^ flip)) for z in range(ring) for c in range(2)
    ]


def ex_send(x, shift, flip):
    return lax.ppermute(x, "expert", ex_pairs(lax.axis_size("expert"), shift, flip))


def chip_gather(x):
    ring = lax.axis_size("expert") // 2
    chip = lax.axis_index("expert") // 2
    return roll_blocks([x] + [ex_send(x, -j, 0) for j in range(1, ring)], chip)


def core_gather(x):
    other = ex_send(x, 0, 1)
    first = lax.axis_index("expert") % 2 == 0
    return jnp.stack([jnp.where(first, x, other), jnp.where(first, other, x)], axis=1)


def expert_sum_scatter(x):
    size = lax.axis_size("expert")
    if not direct(size):
        return lax.psum_scatter(x, "expert", scatter_dimension=1, tiled=True)[:, 0]
    a, _, n, c = x.shape
    ring = size // 2
    me = lax.axis_index("expert")
    core, chip = me % 2, me // 2
    pairs = x.reshape(a, ring, 2, n, c)
    first = core == 0
    mine = jnp.where(first, pairs[:, :, 0], pairs[:, :, 1])
    theirs = jnp.where(first, pairs[:, :, 1], pairs[:, :, 0]).astype(BF)
    half = mine + ex_send(theirs, 0, 1).astype(F32)
    blocks = unroll_blocks(half.astype(BF), chip, axis=1)
    total = lax.dynamic_index_in_dim(half, chip, 1, keepdims=False)
    for j in range(1, ring):
        total = total + ex_send(blocks[j], j, 0).astype(F32)
    return total


def rel_expert(experts):
    size = lax.axis_size("expert")
    if not direct(size):
        return experts
    me = lax.axis_index("expert")
    ring = size // 2
    return 2 * ((experts // 2 - me // 2) % ring) + ((experts % 2) ^ (me % 2))


def pieces_out(x):
    size = lax.axis_size("expert")
    if not direct(size):
        return lax.all_to_all(x, "expert", split_axis=0, concat_axis=0, tiled=True)
    return jnp.stack(
        [x[r] if r == 0 else ex_send(x[r], r // 2, r % 2) for r in range(size)], axis=0
    )


def pieces_back(x):
    size = lax.axis_size("expert")
    if not direct(size):
        return lax.all_to_all(x, "expert", split_axis=0, concat_axis=0, tiled=True)
    return jnp.stack(
        [x[r] if r == 0 else ex_send(x[r], -(r // 2), r % 2) for r in range(size)], axis=0
    )


def dp_rows(x):
    size = lax.axis_size("dp")
    return jnp.stack([x] + [dp_send(x, k) for k in range(1, size)], axis=0)


def dp_rows_sum(x):
    size = lax.axis_size("dp")
    total = x[0].astype(F32)
    for k in range(1, size):
        total = total + dp_send(x[k], -k).astype(F32)
    return total


def on_device(
    tokens,
    cotangent,
    doc_lengths,
    routes,
    rel_bucket,
    norm1,
    attn_in,
    attn_out,
    bias_table,
    norm2,
    router,
    w_gate_up,
    w_down,
):
    rows = tokens.shape[0]
    n_dp = lax.axis_size("dp")
    n_ex = lax.axis_size("expert")
    my_dp = lax.axis_index("dp")
    capacity = max(2, TOP * rows // n_ex + 1)
    slots = -(-(capacity + 1) // 8) * 8
    heads = H // n_dp
    hw = heads * HD
    shard = attn_in.shape[0]

    quarters = attn_in.reshape(shard, 3, n_dp, hw).transpose(2, 0, 1, 3).reshape(n_dp, shard, 3 * hw)
    extra = jnp.concatenate([norm1[:, None], norm2[:, None], router], axis=1)
    n_extra = extra.shape[1]
    width = -(-(3 * hw + n_extra) // 128) * 128
    extra = jnp.pad(extra, ((0, 0), (0, width - 3 * hw - n_extra)))
    quarters = jnp.concatenate(
        [quarters, jnp.broadcast_to(extra[None], (n_dp,) + extra.shape)], axis=2
    )
    mine = unroll_blocks(quarters, my_dp)
    got = [mine[0]] + [dp_send(mine[n_dp - j], -j) for j in range(1, n_dp)]
    row_blocks = roll_blocks(got, my_dp)
    out_t = attn_out.T
    if direct(n_ex):
        w_pack = core_gather(chip_gather(row_blocks)).reshape(n_ex, n_dp, shard, width)
        out_z = chip_gather(out_t)
        out_dp = roll_blocks([out_z] + [dp_send(out_z, -j) for j in range(1, n_dp)], my_dp)
        out_dp = out_dp.transpose(1, 0, 2, 3)
        out_all = core_gather(out_dp).reshape(n_ex, n_dp, shard, D)
    else:
        w_pack = lax.all_gather(row_blocks, "expert", axis=0)
        out_all = lax.all_gather(
            roll_blocks([out_t] + [dp_send(out_t, -j) for j in range(1, n_dp)], my_dp),
            "expert",
            axis=0,
        )
    w_pack = w_pack.transpose(1, 0, 2, 3).reshape(D, width)
    proj_in = w_pack[:, : 3 * hw]
    small = w_pack[:, 3 * hw : 3 * hw + n_extra].astype(F32).T
    gain_one, gain_two = small[0], small[1]
    router_all = w_pack[:, 3 * hw + 2 : 3 * hw + n_extra]
    proj_out = out_all.transpose(1, 0, 2, 3).reshape(D, n_dp, hw)
    proj_out = jnp.concatenate(unroll_blocks(proj_out, my_dp, axis=1), axis=1)

    len_row = jnp.pad(doc_lengths.astype(BF), ((0, 7), (0, D - doc_lengths.shape[1])))
    group = dp_rows(jnp.concatenate([tokens, len_row], axis=0))
    group_lengths = group[:, rows, : doc_lengths.shape[1]].astype(jnp.int32)
    group_in = group[:, :rows].astype(F32)

    route_rel = rel_expert(routes)
    flat_rel = route_rel.reshape(-1)
    route_hits = (flat_rel[:, None] == jnp.arange(n_ex, dtype=jnp.int32)[None, :]).astype(jnp.int32)
    earlier = jnp.cumsum(route_hits, axis=0) - route_hits
    slot_index = jnp.sum(earlier * route_hits, axis=1)
    cell_index = (flat_rel * slots + slot_index).reshape(rows, TOP)
    cells = jnp.arange(n_ex * slots, dtype=jnp.int32)
    place_bool = [cell_index[:, k][:, None] == cells[None, :] for k in range(TOP)]
    place = [p.astype(BF) for p in place_bool]
    place_any = sum(place[1:], place[0])

    def compact(pieces):
        return pieces[:, :capacity].reshape(n_ex * capacity, D)

    def spread(packed):
        return jnp.pad(
            packed.reshape(n_ex, capacity, D), ((0, 0), (0, slots - capacity), (0, 0))
        )

    grad_out = cotangent.astype(F32)
    grad_pieces = mm(place_any, cotangent, ((0,), (0,))).astype(BF).reshape(n_ex, slots, D)
    grad_rows = dp_rows(compact(pieces_out(grad_pieces))).reshape(-1, D)

    inv_one = lax.rsqrt(jnp.mean(group_in * group_in, axis=-1, keepdims=True) + EPSILON)
    normed_one = (group_in * inv_one * gain_one).astype(BF).reshape(n_dp * rows, D)
    qkv = mm(normed_one, proj_in, ((1,), (0,))).astype(BF)
    qkv = qkv.reshape(n_dp, rows, 3, heads, HD).transpose(2, 0, 3, 1, 4)
    queries, keys, values = qkv[0], qkv[1], qkv[2]

    doc_ends = jnp.cumsum(group_lengths, axis=1)
    places = jnp.arange(rows, dtype=jnp.int32)
    doc_index = jnp.sum(
        (places[None, :, None] >= doc_ends[:, None, :]).astype(jnp.int32), axis=2
    )
    allowed = (doc_index[:, :, None] == doc_index[:, None, :]) & (
        places[None, None, :] <= places[None, :, None]
    )
    allowed = allowed[:, None]
    distance = jnp.clip(places[:, None] - places[None, :], 0, LMAX - 1)
    dist_hot = (distance[:, :, None] == jnp.arange(LMAX, dtype=jnp.int32)[None, None, :]).astype(F32)
    bucket_hot = (rel_bucket[:, None] == jnp.arange(NB, dtype=jnp.int32)[None, :]).astype(F32)
    my_bias = lax.dynamic_slice_in_dim(bias_table, my_dp * heads, heads, axis=1)
    bias_dist = jnp.dot(bucket_hot, my_bias, precision=lax.Precision.HIGHEST)
    bias_heads = jnp.einsum("ijr,rh->hij", dist_hot, bias_dist, precision=lax.Precision.HIGHEST)

    scores = (
        jnp.einsum("phid,phjd->phij", queries, keys, preferred_element_type=F32) * SCORE_SCALE
        + bias_heads[None]
    )
    scores = jnp.where(allowed, scores, -jnp.inf)
    row_top = jnp.max(scores, axis=-1, keepdims=True)
    log_total = row_top + jnp.log(jnp.sum(jnp.exp(scores - row_top), axis=-1, keepdims=True))
    attn_probs = jnp.exp(scores - log_total)
    attn_weights = attn_probs.astype(BF)
    context_heads = jnp.einsum("phij,phjd->pihd", attn_weights, values, preferred_element_type=F32)
    context_heads = context_heads.reshape(n_dp, rows, hw).astype(BF)
    context = jnp.concatenate(
        [context_heads[0]] + [dp_send(context_heads[k], -k) for k in range(1, n_dp)], axis=1
    )

    inputs = tokens.astype(F32)
    residual = inputs + mm(context, proj_out, ((1,), (1,)))
    inv_two = lax.rsqrt(jnp.mean(residual * residual, axis=-1, keepdims=True) + EPSILON)
    normed_two = (residual * inv_two * gain_two).astype(BF)
    logits = mm(normed_two, router_all, ((1,), (0,)))
    route_picks = (
        routes[:, :, None] == jnp.arange(n_ex, dtype=jnp.int32)[None, None, :]
    ).astype(F32)
    chosen = jnp.sum(route_picks * logits[:, None, :], axis=2)
    chosen_exp = jnp.exp(chosen - jnp.max(chosen, axis=1, keepdims=True))
    route_weight = chosen_exp / jnp.sum(chosen_exp, axis=1, keepdims=True)

    cell_weight = sum(
        jnp.sum(jnp.where(place_bool[k], route_weight[:, k][:, None], 0.0), axis=0)
        for k in range(TOP)
    ).reshape(n_ex, slots)
    part_hi = cell_weight.astype(BF)
    rest = cell_weight - part_hi.astype(F32)
    part_mid = rest.astype(BF)
    part_lo = (rest - part_mid.astype(F32)).astype(BF)
    weight_row = jnp.concatenate([part_hi, part_mid, part_lo], axis=1)
    weight_row = jnp.pad(weight_row, ((0, 0), (0, D - 3 * slots)))
    row_pieces = mm(place_any, normed_two, ((0,), (0,))).astype(BF).reshape(n_ex, slots, D)
    slot_ids = jnp.arange(slots, dtype=jnp.int32)[None, :, None]
    row_pieces = jnp.where(slot_ids == capacity, weight_row[:, None, :], row_pieces)
    arrived = pieces_out(row_pieces)
    n_cells = n_ex * capacity
    sent = jnp.concatenate([compact(arrived), arrived[:, capacity]], axis=0)
    everything = dp_rows(sent)
    x_rows = everything[:, :n_cells].reshape(n_dp * n_cells, D)
    weights_in = everything[:, n_cells:, : 3 * slots].astype(F32).reshape(n_dp, n_ex, 3, slots)
    weights_in = weights_in[:, :, 0] + weights_in[:, :, 1] + weights_in[:, :, 2]
    weights_in = weights_in[:, :, :capacity].reshape(n_dp * n_cells, 1)

    units = w_down.shape[1]
    w_gu = w_gate_up[0].reshape(D, 2 * units)
    w_dn = w_down[0]
    gate_up = mm(x_rows, w_gu, ((1,), (0,)))
    gate, up = gate_up[:, :units], gate_up[:, units:]
    activated, derivative = gelu_parts(gate)
    hidden = (activated * up).astype(BF)
    produced = mm(hidden, w_dn, ((1,), (0,))).astype(BF).reshape(n_dp, n_cells, D)
    returned = pieces_back(spread(dp_rows_sum(produced).astype(BF))).reshape(n_ex * slots, D)

    d_rows_in = (weights_in * grad_rows.astype(F32)).astype(BF)
    d_hidden = mm(d_rows_in, w_dn, ((1,), (1,)))
    d_gate_up = jnp.concatenate([d_hidden * up * derivative, d_hidden * activated], axis=1).astype(
        BF
    )
    d_rows_out = mm(d_gate_up, w_gu, ((1,), (1,))).astype(BF).reshape(n_dp, n_cells, D)
    d_returned = pieces_back(spread(dp_rows_sum(d_rows_out).astype(BF))).reshape(n_ex * slots, D)
    d_w_gate_up = mm(x_rows, d_gate_up, ((0,), (0,))).reshape(1, D, 2, units)
    d_w_down = mm(hidden, d_rows_in, ((0,), (0,)))[None]

    expert_out = [mm(p, returned, ((1,), (0,))) for p in place]
    output = (
        residual + sum(route_weight[:, k][:, None] * expert_out[k] for k in range(TOP))
    ).astype(BF)
    d_route_weight = jnp.stack([jnp.sum(grad_out * e, axis=1) for e in expert_out], axis=1)
    route_delta = d_route_weight - jnp.sum(d_route_weight * route_weight, axis=1, keepdims=True)
    d_logits = jnp.sum(route_picks * (route_weight * route_delta)[:, :, None], axis=1).astype(BF)
    d_router_part = mm(normed_two, d_logits, ((0,), (0,)))
    d_normed_two = mm(place_any, d_returned, ((1,), (0,))) + mm(
        d_logits, router_all, ((1,), (1,))
    )
    scaled = gain_two * d_normed_two
    d_norm2_part = jnp.sum(d_normed_two * residual * inv_two, axis=0)
    d_residual = (
        grad_out
        + inv_two * scaled
        - residual
        * (inv_two * inv_two * inv_two)
        * jnp.mean(scaled * residual, axis=-1, keepdims=True)
    )
    d_residual_b = d_residual.astype(BF)
    d_context = mm(d_residual_b, proj_out, ((1,), (0,))).astype(BF)
    d_ctx_blocks = d_context.reshape(rows, n_dp, hw)
    d_heads = jnp.stack(
        [d_ctx_blocks[:, 0]] + [dp_send(d_ctx_blocks[:, k], k) for k in range(1, n_dp)], axis=0
    )
    d_heads = d_heads.reshape(n_dp, rows, heads, HD)
    d_out_part = mm(d_residual_b, context, ((0,), (0,)))
    d_out_rows = expert_sum_scatter(d_out_part.reshape(n_dp, n_ex, shard, D))
    d_out_rows = d_out_rows.astype(BF).reshape(n_dp, shard, n_dp, hw)
    d_out_rows = roll_blocks([d_out_rows[:, :, j] for j in range(n_dp)], my_dp)
    d_out_rows = d_out_rows.transpose(1, 2, 0, 3).reshape(n_dp, shard, D)
    out_blocks = unroll_blocks(d_out_rows, my_dp)
    d_attn_out = out_blocks[0].astype(F32)
    for k in range(1, n_dp):
        d_attn_out = d_attn_out + dp_send(out_blocks[k], k).astype(F32)
    d_attn_out = d_attn_out.T

    d_probs = jnp.einsum("pihd,phjd->phij", d_heads, values, preferred_element_type=F32)
    row_delta = jnp.sum(attn_probs * d_probs, axis=-1, keepdims=True)
    d_scores = jnp.where(allowed, attn_probs * (d_probs - row_delta), 0.0)
    d_scores_b = d_scores.astype(BF)
    d_queries = (
        jnp.einsum("phij,phjd->pihd", d_scores_b, keys, preferred_element_type=F32) * SCORE_SCALE
    ).astype(BF)
    d_keys = (
        jnp.einsum("phij,phid->pjhd", d_scores_b, queries, preferred_element_type=F32)
        * SCORE_SCALE
    ).astype(BF)
    d_values = jnp.einsum(
        "phij,pihd->pjhd", attn_weights, d_heads, preferred_element_type=F32
    ).astype(BF)
    d_qkv = jnp.concatenate(
        [g.reshape(n_dp * rows, hw) for g in (d_queries, d_keys, d_values)], axis=1
    )
    d_normed_part = mm(d_qkv, proj_in, ((1,), (1,))).reshape(n_dp, rows, D)
    d_norm1_part = jnp.sum(d_normed_part * group_in * inv_one, axis=(0, 1))
    d_in_part = mm(normed_one, d_qkv, ((0,), (0,)))
    extra_part = jnp.concatenate(
        [jnp.stack([d_norm1_part, d_norm2_part], axis=1), d_router_part], axis=1
    )
    extra_part = jnp.pad(extra_part, ((0, 0), (0, width - 3 * hw - n_extra)))
    d_pack = jnp.concatenate([d_in_part, extra_part], axis=1)
    d_pack_rows = expert_sum_scatter(d_pack.reshape(n_dp, n_ex, shard, width)).astype(BF)
    pack_blocks = unroll_blocks(d_pack_rows, my_dp)
    got = [pack_blocks[0]] + [dp_send(pack_blocks[n_dp - j], -j) for j in range(1, n_dp)]
    d_pack_all = roll_blocks(got, my_dp).astype(F32)
    d_attn_in = (
        d_pack_all[:, :, : 3 * hw].reshape(n_dp, shard, 3, hw).transpose(1, 2, 0, 3)
    ).reshape(shard, 3 * n_dp * hw)
    d_extra = jnp.sum(d_pack_all[:, :, 3 * hw : 3 * hw + n_extra], axis=0)
    d_norm1, d_norm2, d_router = d_extra[:, 0], d_extra[:, 1], d_extra[:, 2:]

    d_normed_one = dp_rows_sum(d_normed_part.astype(BF))
    inv_mine = inv_one[0]
    scaled_one = gain_one * d_normed_one
    d_tokens = (
        d_residual
        + inv_mine * scaled_one
        - inputs
        * (inv_mine * inv_mine * inv_mine)
        * jnp.mean(scaled_one * inputs, axis=-1, keepdims=True)
    )

    d_dist = jnp.einsum(
        "hij,ijr->hr", jnp.sum(d_scores, axis=0), dist_hot, precision=lax.Precision.HIGHEST
    )
    d_bias = jnp.dot(d_dist, bucket_hot, precision=lax.Precision.HIGHEST)
    step = 1
    while step < n_ex:
        d_bias = d_bias + lax.ppermute(d_bias, "expert", [(i, i ^ step) for i in range(n_ex)])
        step *= 2
    d_bias_all = roll_blocks(
        [d_bias] + [dp_send(d_bias, -j) for j in range(1, n_dp)], my_dp
    )
    d_bias_table = d_bias_all.reshape(H, NB).T

    return (
        output,
        d_tokens,
        d_norm1,
        d_attn_in,
        d_attn_out,
        d_bias_table,
        d_norm2,
        d_router,
        d_w_gate_up,
        d_w_down,
    )


def solution(mesh):
    both = ("dp", "expert")
    in_specs = (
        P(both, None),
        P(both, None),
        P(both, None),
        P(both, None),
        P(),
        P(both),
        P(both, None),
        P(None, both),
        P(),
        P(both),
        P(both, None),
        P("expert", None, None, "dp"),
        P("expert", "dp", None),
    )
    out_specs = (
        P(both, None),
        P(both, None),
        P(both),
        P(both, None),
        P(None, both),
        P(),
        P(both),
        P(both, None),
        P("expert", None, None, "dp"),
        P("expert", "dp", None),
    )
    return jax.shard_map(
        on_device, mesh=mesh, in_specs=in_specs, out_specs=out_specs, check_vma=False
    )
```

```python
import jax
import jax.numpy as jnp
from jax import lax
from jax.experimental import pallas as pl
from jax.experimental.pallas import tpu as pltpu
from jax.sharding import PartitionSpec as P

D = 768
H = 12
HD = 64
TOP = 2
NB = 32
LMAX = 96

EPSILON = 1e-06
GELU_COEF = 0.7978845608028654
GELU_CUBE = 0.044715
SCORE_SCALE = 0.125

BF = jnp.bfloat16
F32 = jnp.float32


def gelu_parts(gate_in):
    inner_arg = GELU_COEF * (gate_in + GELU_CUBE * gate_in * gate_in * gate_in)
    tanh_part = jnp.tanh(inner_arg)
    result = 0.5 * gate_in * (1.0 + tanh_part)
    derivative = 0.5 * (1.0 + tanh_part) + 0.5 * gate_in * (
        1.0 - tanh_part * tanh_part
    ) * GELU_COEF * (1.0 + 3.0 * GELU_CUBE * gate_in * gate_in)
    return (result, derivative)


def mm(a, b, dims):
    return lax.dot_general(a, b, (dims, ((), ())), preferred_element_type=F32)


def reorder(blocks, me):
    bit = 1
    while bit < len(blocks):
        on = (me & bit) != 0
        blocks = [jnp.where(on, blocks[q ^ bit], blocks[q]) for q in range(len(blocks))]
        bit *= 2
    return blocks


def with_dp(x, k):
    size = lax.axis_size("dp")
    return lax.ppermute(x, "dp", [(i, i ^ k) for i in range(size)]) if k else x


def with_expert(x, k):
    size = lax.axis_size("expert")
    return lax.ppermute(x, "expert", [(i, i ^ k) for i in range(size)]) if k else x


def n_dp_of():
    return lax.axis_size("dp")


def share_dp(x):
    return [with_dp(x, k) for k in range(n_dp_of())]


def swap_dp(blocks):
    return [with_dp(x, k) for k, x in enumerate(blocks)]


def sum_dp(blocks):
    total = blocks[0].astype(F32)
    for k in range(1, len(blocks)):
        total = total + with_dp(blocks[k], k).astype(F32)
    return total


def direct():
    return lax.axis_size("expert") <= 8


def share_expert(x):
    size = lax.axis_size("expert")
    if not direct():
        every = lax.all_gather(x, "expert", axis=0)
        return [every[e] for e in range(size)]
    chips = [with_expert(x, 2 * j) for j in range(size // 2)]
    return finish_expert(chips)


def finish_expert(chips):
    me = lax.axis_index("expert")
    own = jnp.stack(chips)
    other = with_expert(own, 1)
    first = me % 2 == 0
    even = jnp.where(first, own, other)
    odd = jnp.where(first, other, own)
    n = len(chips)
    even = reorder([even[j] for j in range(n)], me // 2)
    odd = reorder([odd[j] for j in range(n)], me // 2)
    return [x for pair in zip(even, odd) for x in pair]


def expert_sum_scatter(x):
    a, size, n, c = x.shape
    if not direct():
        return lax.psum_scatter(x, "expert", scatter_dimension=1, tiled=True)[:, 0]
    pairs = x.reshape(a, size // 2, 2, n, c)
    me = lax.axis_index("expert")
    first = me % 2 == 0
    mine = jnp.where(first, pairs[:, :, 0], pairs[:, :, 1])
    theirs = jnp.where(first, pairs[:, :, 1], pairs[:, :, 0]).astype(BF)
    theirs = with_expert(theirs, 1)
    half = mine + theirs.astype(F32)
    blocks = reorder([half[:, z] for z in range(size // 2)], me // 2)
    total = blocks[0]
    got = [with_expert(blocks[j].astype(BF), 2 * j) for j in range(1, size // 2)]
    for x in got:
        total = total + x.astype(F32)
    return total


class Cells:
    def __init__(self, capacity):
        size = lax.axis_size("expert")
        self.size, self.part = size, capacity + 1
        self.direct = direct()
        if self.direct:
            self.chips = size // 2
            self.cut = self.part // 8 * 8
            self.block = -(-2 * self.part // 8) * 8
            self.tail = self.block - self.cut
            self.near = self.chips * self.block
            self.total = self.near + self.chips * self.tail
            self.rows = self.near
            self.marks = (capacity, self.part + capacity)
        else:
            self.block = -(-self.part // 8) * 8
            self.total = self.rows = size * self.block
            self.marks = (capacity,)

    def index(self, routes, slot):
        if not self.direct:
            return routes * self.block + slot
        rel = routes ^ lax.axis_index("expert")
        chip, other = rel // 2, rel % 2
        near = chip * self.block + slot
        far = self.near + chip * self.tail + self.part - self.cut + slot
        return jnp.where(other == 0, near, far)

    def mark_rows(self, packed, weights):
        def write(rows, values, first, mark):
            n, height = values.shape
            values = jnp.pad(values, ((0, 0), (first, 128 - height - first)))
            hi = values.astype(BF)
            rest = values - hi.astype(F32)
            mid = rest.astype(BF)
            lo = (rest - mid.astype(F32)).astype(BF)
            line = jnp.pad(jnp.concatenate([hi, mid, lo], axis=1), ((0, 0), (0, D - 384)))
            rows = rows.reshape(n, height, D)
            at = jnp.arange(height, dtype=jnp.int32)[None, :, None] == mark
            return jnp.where(at, line[:, None, :], rows).reshape(n * height, D)

        if not self.direct:
            return [write(packed[0], weights.reshape(self.size, self.block), 0, self.marks[0])]
        near, far = weights[: self.near], weights[self.near :]
        return [
            write(packed[0], near.reshape(self.chips, self.block), 0, self.marks[0]),
            write(
                packed[1], far.reshape(self.chips, self.tail), self.cut, self.marks[1] - self.cut
            ),
        ]

    def read_marks(self, rows):
        rows = rows.reshape(-1, self.block, D)
        line = sum(rows[:, m, p * 128 : (p + 1) * 128].astype(F32) for m in self.marks for p in range(3))
        return line[:, : self.block].reshape(-1, 1)

    def cuts(self, packed):
        return [packed[..., : self.near], packed[..., self.near :]] if self.direct else [packed]

    def dispatch(self, packed):
        if not self.direct:
            x = packed[0].reshape(self.size, self.block, D)
            x = lax.all_to_all(x, "expert", split_axis=0, concat_axis=0, tiled=True)
            return x.reshape(self.rows, D)
        far = with_expert(packed[1], 1).reshape(self.chips, self.tail, D)
        both = packed[0].reshape(self.chips, self.block, D) + jnp.pad(
            far, ((0, 0), (self.cut, 0), (0, 0))
        )
        got = [with_expert(both[j], 2 * j) for j in range(self.chips)]
        return jnp.concatenate(got, axis=0)

    def collect(self, rows):
        if not self.direct:
            x = rows.reshape(self.size, self.block, D)
            x = lax.all_to_all(x, "expert", split_axis=0, concat_axis=0, tiled=True)
            return [x.reshape(self.total, D)]
        x = rows.reshape(self.chips, self.block, D)
        back = [with_expert(x[j], 2 * j) for j in range(self.chips)]
        far = with_expert(jnp.concatenate([y[self.cut :] for y in back], axis=0), 1)
        return [jnp.concatenate(back, axis=0), far]


def pack_quarters(attn_in, extra, me, n_dp, hw, width):
    shard = attn_in.shape[0]

    def kernel(me_ref, w_ref, extra_ref, *out_refs):
        me = me_ref[0]
        w = w_ref[...].astype(F32)
        last = extra_ref[...].astype(F32)
        for q in range(n_dp):
            cols = [w[:, g * D + q * hw : g * D + (q + 1) * hw] for g in range(3)]
            block = jnp.concatenate(cols + [last], axis=1).astype(BF)
            for k in range(n_dp):

                @pl.when((me ^ k) == q)
                def _():
                    out_refs[k][...] = block

    whole = pl.BlockSpec(memory_space=pltpu.VMEM)
    return pl.pallas_call(
        kernel,
        out_shape=[jax.ShapeDtypeStruct((shard, width), BF)] * n_dp,
        in_specs=[pl.BlockSpec(memory_space=pltpu.SMEM), whole, whole],
        out_specs=[whole] * n_dp,
        name="pack_quarters",
    )(me.reshape(1).astype(jnp.int32), attn_in, extra)


def weight_grad(x_a, x_b, y_a, y_b, parts):
    m, n = x_a.shape[1], y_a.shape[1]
    tile = 256
    part = n // parts

    def kernel(xa, xb, ya, yb, out):
        both = mm(xa[...], ya[...], ((0,), (0,))) + mm(xb[...], yb[...], ((0,), (0,)))
        if parts == 1:
            out[...] = both
        else:
            for g in range(parts):
                out[:, g, :] = both[:, g * part : (g + 1) * part]

    def column(x):
        return pl.BlockSpec((x.shape[0], tile), lambda i: (0, i))

    def whole(y):
        return pl.BlockSpec(y.shape, lambda i: (0, 0))

    if parts == 1:
        shape, out_spec = (m, n), pl.BlockSpec((tile, n), lambda i: (i, 0))
    else:
        shape = (m, parts, part)
        out_spec = pl.BlockSpec((tile, parts, part), lambda i: (i, 0, 0))
    return pl.pallas_call(
        kernel,
        grid=(m // tile,),
        out_shape=jax.ShapeDtypeStruct(shape, F32),
        in_specs=[column(x_a), column(x_b), whole(y_a), whole(y_b)],
        out_specs=out_spec,
        name="weight_grad",
    )(x_a, x_b, y_a, y_b)


def on_device(
    tokens,
    cotangent,
    doc_lengths,
    routes,
    rel_bucket,
    norm1,
    attn_in,
    attn_out,
    bias_table,
    norm2,
    router,
    w_gate_up,
    w_down,
):
    rows = tokens.shape[0]
    n_dp = lax.axis_size("dp")
    n_ex = lax.axis_size("expert")
    my_dp = lax.axis_index("dp")
    capacity = max(2, TOP * rows // n_ex + 1)
    cells = Cells(capacity)
    heads = H // n_dp
    hw = heads * HD
    shard = attn_in.shape[0]

    extra = jnp.concatenate([norm1[:, None], norm2[:, None], router], axis=1)
    n_extra = extra.shape[1]
    width = -(-(3 * hw + n_extra) // 128) * 128
    extra = jnp.pad(extra, ((0, 0), (0, width - 3 * hw - n_extra)))
    sent = pack_quarters(attn_in, extra, my_dp, n_dp, hw, width)
    got = swap_dp(sent)
    w_all = share_expert(jnp.stack(reorder(got, my_dp)))
    w_pack = jnp.stack(w_all, axis=1).reshape(D, width)
    small = w_pack[:, 3 * hw : 3 * hw + n_extra].astype(F32).T
    gain_one, gain_two = small[0], small[1]
    router_all = w_pack[:, 3 * hw + 2 : 3 * hw + n_extra]
    if direct():
        out_z = jnp.stack([with_expert(attn_out.T, 2 * j) for j in range(n_ex // 2)])
        out_dp = share_dp(out_z)
        out_dp = jnp.stack(reorder(out_dp, my_dp), axis=1)
        proj_out = finish_expert([out_dp[j] for j in range(n_ex // 2)])
    else:
        proj_out = share_expert(jnp.stack(reorder(share_dp(attn_out.T), my_dp)))
    proj_out = jnp.stack(proj_out, axis=1).reshape(D, D)

    len_row = jnp.pad(doc_lengths.astype(BF), ((0, 7), (0, D - doc_lengths.shape[1])))
    group = jnp.stack(share_dp(jnp.concatenate([tokens, len_row], axis=0)))
    group_lengths = group[:, rows, : doc_lengths.shape[1]].astype(jnp.int32)
    group_in = group[:, :rows].astype(F32)

    flat_routes = routes.reshape(-1)
    route_hits = (flat_routes[:, None] == jnp.arange(n_ex, dtype=jnp.int32)[None, :]).astype(
        jnp.int32
    )
    earlier = jnp.cumsum(route_hits, axis=0) - route_hits
    slot_index = jnp.sum(earlier * route_hits, axis=1).reshape(rows, TOP)
    cell_index = cells.index(routes, slot_index)
    cell_ids = jnp.arange(cells.total, dtype=jnp.int32)
    place_bool = [cell_index[:, k][:, None] == cell_ids[None, :] for k in range(TOP)]
    place = [p.astype(BF) for p in place_bool]
    place_any = sum(place[1:], place[0])

    def packed(x):
        return [mm(p, x, ((0,), (0,))).astype(BF) for p in cells.cuts(place_any)]

    def unpacked(p, parts):
        return sum(mm(q, x, ((1,), (0,))) for q, x in zip(cells.cuts(p), parts))

    grad_out = cotangent.astype(F32)
    grad_rows = packed(cotangent)
    grad_rows = cells.dispatch(grad_rows)
    grad_rows = share_dp(grad_rows)

    inv_one = lax.rsqrt(jnp.mean(group_in * group_in, axis=-1, keepdims=True) + EPSILON)
    normed_one = (group_in * inv_one * gain_one).astype(BF).reshape(n_dp * rows, D)
    qkv = mm(normed_one, w_pack, ((1,), (0,)))[:, : 3 * hw].astype(BF)
    qkv = qkv.reshape(n_dp, rows, 3, heads, HD).transpose(2, 0, 3, 1, 4)
    queries, keys, values = qkv[0], qkv[1], qkv[2]

    doc_ends = jnp.cumsum(group_lengths, axis=1)
    places = jnp.arange(rows, dtype=jnp.int32)
    doc_index = jnp.sum(
        (places[None, :, None] >= doc_ends[:, None, :]).astype(jnp.int32), axis=2
    )
    allowed = (doc_index[:, :, None] == doc_index[:, None, :]) & (
        places[None, None, :] <= places[None, :, None]
    )
    allowed = allowed[:, None]
    distance = jnp.clip(places[:, None] - places[None, :], 0, LMAX - 1)
    dist_hot = (distance[:, :, None] == jnp.arange(LMAX, dtype=jnp.int32)[None, None, :]).astype(F32)
    bucket_hot = (rel_bucket[:, None] == jnp.arange(NB, dtype=jnp.int32)[None, :]).astype(F32)
    my_bias = lax.dynamic_slice_in_dim(bias_table, my_dp * heads, heads, axis=1)
    bias_dist = jnp.dot(bucket_hot, my_bias, precision=lax.Precision.HIGHEST)
    bias_heads = jnp.einsum("ijr,rh->hij", dist_hot, bias_dist, precision=lax.Precision.HIGHEST)

    scores = (
        jnp.einsum("phid,phjd->phij", queries, keys, preferred_element_type=F32) * SCORE_SCALE
        + bias_heads[None]
    )
    scores = jnp.where(allowed, scores, -jnp.inf)
    row_top = jnp.max(scores, axis=-1, keepdims=True)
    log_total = row_top + jnp.log(jnp.sum(jnp.exp(scores - row_top), axis=-1, keepdims=True))
    attn_probs = jnp.exp(scores - log_total)
    attn_weights = attn_probs.astype(BF)
    context_heads = jnp.einsum("phij,phjd->pihd", attn_weights, values, preferred_element_type=F32)
    context_heads = context_heads.reshape(n_dp, rows, hw).astype(BF)
    context = swap_dp([context_heads[k] for k in range(n_dp)])
    context = reorder(context, my_dp)
    context = jnp.concatenate(context, axis=1)

    inputs = tokens.astype(F32)
    residual = inputs + mm(context, proj_out, ((1,), (1,)))
    inv_two = lax.rsqrt(jnp.mean(residual * residual, axis=-1, keepdims=True) + EPSILON)
    normed_two = (residual * inv_two * gain_two).astype(BF)
    logits = mm(normed_two, router_all, ((1,), (0,)))
    route_picks = (
        routes[:, :, None] == jnp.arange(n_ex, dtype=jnp.int32)[None, None, :]
    ).astype(F32)
    chosen = jnp.sum(route_picks * logits[:, None, :], axis=2)
    chosen_exp = jnp.exp(chosen - jnp.max(chosen, axis=1, keepdims=True))
    route_weight = chosen_exp / jnp.sum(chosen_exp, axis=1, keepdims=True)

    cell_weight = sum(
        jnp.sum(jnp.where(place_bool[k], route_weight[:, k][:, None], 0.0), axis=0)
        for k in range(TOP)
    )
    arrived = cells.dispatch(cells.mark_rows(packed(normed_two), cell_weight))
    x_blocks = [with_dp(arrived, k) for k in range(n_dp - 1)]
    x_blocks.append(with_dp(arrived, n_dp - 1))

    units = w_down.shape[1]
    w_gu = w_gate_up[0].reshape(D, 2 * units)
    w_dn = w_down[0]

    def expert(x_list, grad_list):
        x = jnp.concatenate(x_list, axis=0)
        weights_in = cells.read_marks(x)
        gate_up = mm(x, w_gu, ((1,), (0,)))
        gate, up = gate_up[:, :units], gate_up[:, units:]
        activated, derivative = gelu_parts(gate)
        hidden = (activated * up).astype(BF)
        produced = mm(hidden, w_dn, ((1,), (0,))).astype(BF)
        d_rows_in = (weights_in * jnp.concatenate(grad_list, axis=0).astype(F32)).astype(BF)
        d_hidden = mm(d_rows_in, w_dn, ((1,), (1,)))
        d_gate_up = jnp.concatenate(
            [d_hidden * up * derivative, d_hidden * activated], axis=1
        ).astype(BF)
        d_rows_out = mm(d_gate_up, w_gu, ((1,), (1,))).astype(BF)
        blocks = (len(x_list), cells.rows, D)
        return (
            list(produced.reshape(blocks)),
            list(d_rows_out.reshape(blocks)),
            (x, d_gate_up, hidden, d_rows_in),
        )

    first_out = expert(x_blocks[:-1], grad_rows[:-1])
    last_out = expert(x_blocks[-1:], grad_rows[-1:])

    def sum_back(index):
        blocks = first_out[index]
        total = blocks[0].astype(F32)
        got = [with_dp(blocks[k], k) for k in range(1, n_dp - 1)]
        got.append(with_dp(last_out[index][0], n_dp - 1))
        for x in got:
            total = total + x.astype(F32)
        return total.astype(BF)

    returned = cells.collect(sum_back(0))
    d_returned = cells.collect(sum_back(1))
    (x_a, dgu_a, hid_a, dri_a), (x_b, dgu_b, hid_b, dri_b) = first_out[2], last_out[2]
    d_w_gate_up = weight_grad(x_a, x_b, dgu_a, dgu_b, 2)[None]
    d_w_down = weight_grad(hid_a, hid_b, dri_a, dri_b, 1)[None]

    expert_out = [unpacked(p, returned) for p in place]
    output = (
        residual + sum(route_weight[:, k][:, None] * expert_out[k] for k in range(TOP))
    ).astype(BF)
    d_route_weight = jnp.stack([jnp.sum(grad_out * e, axis=1) for e in expert_out], axis=1)
    route_delta = d_route_weight - jnp.sum(d_route_weight * route_weight, axis=1, keepdims=True)
    d_logits = jnp.sum(route_picks * (route_weight * route_delta)[:, :, None], axis=1).astype(BF)
    d_router_part = mm(normed_two, d_logits, ((0,), (0,)))
    d_normed_two = unpacked(place_any, d_returned) + mm(d_logits, router_all, ((1,), (1,)))
    scaled = gain_two * d_normed_two
    d_norm2_part = jnp.sum(d_normed_two * residual * inv_two, axis=0)
    d_residual = (
        grad_out
        + inv_two * scaled
        - residual
        * (inv_two * inv_two * inv_two)
        * jnp.mean(scaled * residual, axis=-1, keepdims=True)
    )
    d_residual_b = d_residual.astype(BF)
    d_context = mm(d_residual_b, proj_out, ((1,), (0,))).astype(BF)
    d_ctx = reorder([d_context[:, q * hw : (q + 1) * hw] for q in range(n_dp)], my_dp)
    d_heads = jnp.stack(swap_dp(d_ctx)).reshape(n_dp, rows, heads, HD)
    d_out_part = mm(d_residual_b, context, ((0,), (0,)))
    d_out_rows = expert_sum_scatter(d_out_part.reshape(n_dp, n_ex, shard, D)).astype(BF)

    d_probs = jnp.einsum("pihd,phjd->phij", d_heads, values, preferred_element_type=F32)
    row_delta = jnp.sum(attn_probs * d_probs, axis=-1, keepdims=True)
    d_scores = jnp.where(allowed, attn_probs * (d_probs - row_delta), 0.0)
    d_scores_b = d_scores.astype(BF)
    d_queries = (
        jnp.einsum("phij,phjd->pihd", d_scores_b, keys, preferred_element_type=F32) * SCORE_SCALE
    ).astype(BF)
    d_keys = (
        jnp.einsum("phij,phid->pjhd", d_scores_b, queries, preferred_element_type=F32)
        * SCORE_SCALE
    ).astype(BF)
    d_values = jnp.einsum(
        "phij,pihd->pjhd", attn_weights, d_heads, preferred_element_type=F32
    ).astype(BF)
    d_qkv = jnp.concatenate(
        [g.reshape(n_dp * rows, hw) for g in (d_queries, d_keys, d_values)]
        + [jnp.zeros((n_dp * rows, width - 3 * hw), BF)],
        axis=1,
    )
    d_normed_part = mm(d_qkv, w_pack, ((1,), (1,))).reshape(n_dp, rows, D)
    d_norm1_part = jnp.sum(d_normed_part * group_in * inv_one, axis=(0, 1))
    d_in_part = mm(normed_one, d_qkv, ((0,), (0,)))
    extra_part = jnp.concatenate(
        [jnp.stack([d_norm1_part, d_norm2_part], axis=1), d_router_part], axis=1
    )
    extra_part = jnp.pad(extra_part, ((0, 0), (3 * hw, width - 3 * hw - n_extra)))
    d_pack = d_in_part + extra_part
    d_pack_rows = expert_sum_scatter(d_pack.reshape(n_dp, n_ex, shard, width)).astype(BF)

    d_dist = jnp.einsum(
        "hij,ijr->hr", jnp.sum(d_scores, axis=0), dist_hot, precision=lax.Precision.HIGHEST
    )
    d_bias = jnp.dot(d_dist, bucket_hot, precision=lax.Precision.HIGHEST)
    d_bias = jnp.pad(d_bias.reshape(1, heads * NB), ((0, 0), (0, 128 - heads * NB)))
    step = 1
    while step < n_ex:
        d_bias = d_bias + with_expert(d_bias, step)
        step *= 2
    bias_hi = d_bias.astype(BF)
    bias_lo = (d_bias - bias_hi.astype(F32)).astype(BF)
    bias_row = jnp.pad(jnp.concatenate([bias_hi, bias_lo], axis=1), ((0, 0), (0, width + D - 256)))

    last = jnp.concatenate([d_pack_rows, d_out_rows], axis=2)
    last = [
        jnp.concatenate([x, bias_row], axis=0)
        for x in reorder([last[q] for q in range(n_dp)], my_dp)
    ]
    last = swap_dp(last)
    last = jnp.stack(reorder(last, my_dp)).astype(F32)
    d_attn_in = (
        last[:, :shard, : 3 * hw].reshape(n_dp, shard, 3, hw).transpose(1, 2, 0, 3)
    ).reshape(shard, 3 * n_dp * hw)
    d_extra = jnp.sum(last[:, :shard, 3 * hw : 3 * hw + n_extra], axis=0)
    d_norm1, d_norm2, d_router = d_extra[:, 0], d_extra[:, 1], d_extra[:, 2:]
    d_attn_out = jnp.sum(last[:, :shard, width:], axis=0).T
    d_bias = last[:, shard, :128] + last[:, shard, 128:256]
    d_bias_table = d_bias[:, : heads * NB].reshape(H, NB).T

    d_normed_b = d_normed_part.astype(BF)
    d_normed_one = sum_dp([d_normed_b[k] for k in range(n_dp)])
    inv_mine = inv_one[0]
    scaled_one = gain_one * d_normed_one
    d_tokens = (
        d_residual
        + inv_mine * scaled_one
        - inputs
        * (inv_mine * inv_mine * inv_mine)
        * jnp.mean(scaled_one * inputs, axis=-1, keepdims=True)
    )

    return (
        output,
        d_tokens,
        d_norm1,
        d_attn_in,
        d_attn_out,
        d_bias_table,
        d_norm2,
        d_router,
        d_w_gate_up,
        d_w_down,
    )


def solution(mesh):
    both = ("dp", "expert")
    in_specs = (
        P(both, None),
        P(both, None),
        P(both, None),
        P(both, None),
        P(),
        P(both),
        P(both, None),
        P(None, both),
        P(),
        P(both),
        P(both, None),
        P("expert", None, None, "dp"),
        P("expert", "dp", None),
    )
    out_specs = (
        P(both, None),
        P(both, None),
        P(both),
        P(both, None),
        P(None, both),
        P(),
        P(both),
        P(both, None),
        P("expert", None, None, "dp"),
        P("expert", "dp", None),
    )

    return jax.shard_map(
        on_device, mesh=mesh, in_specs=in_specs, out_specs=out_specs, check_vma=False
    )
```

```python
import jax
import jax.numpy as jnp
from jax import lax
from jax.experimental import pallas as pl
from jax.experimental.pallas import tpu as pltpu
from jax.sharding import PartitionSpec as P

D = 768
H = 12
HD = 64
TOP = 2
NB = 32
LMAX = 96

EPSILON = 1e-06
GELU_COEF = 0.7978845608028654
GELU_CUBE = 0.044715
SCORE_SCALE = 0.125

BF = jnp.bfloat16
F32 = jnp.float32


def gelu_parts(gate_in):
    inner_arg = GELU_COEF * (gate_in + GELU_CUBE * gate_in * gate_in * gate_in)
    tanh_part = jnp.tanh(inner_arg)
    result = 0.5 * gate_in * (1.0 + tanh_part)
    derivative = 0.5 * (1.0 + tanh_part) + 0.5 * gate_in * (
        1.0 - tanh_part * tanh_part
    ) * GELU_COEF * (1.0 + 3.0 * GELU_CUBE * gate_in * gate_in)
    return (result, derivative)


def mm(a, b, dims):
    return lax.dot_general(a, b, (dims, ((), ())), preferred_element_type=F32)


def reorder(blocks, me):
    bit = 1
    while bit < len(blocks):
        on = (me & bit) != 0
        blocks = [jnp.where(on, blocks[q ^ bit], blocks[q]) for q in range(len(blocks))]
        bit *= 2
    return blocks


def with_dp(x, k):
    size = lax.axis_size("dp")
    return lax.ppermute(x, "dp", [(i, i ^ k) for i in range(size)]) if k else x


def with_expert(x, k):
    size = lax.axis_size("expert")
    return lax.ppermute(x, "expert", [(i, i ^ k) for i in range(size)]) if k else x


def n_dp_of():
    return lax.axis_size("dp")


def share_dp(x):
    return [with_dp(x, k) for k in range(n_dp_of())]


def swap_dp(blocks):
    return [with_dp(x, k) for k, x in enumerate(blocks)]


def sum_dp(blocks):
    total = blocks[0].astype(F32)
    for k in range(1, len(blocks)):
        total = total + with_dp(blocks[k], k).astype(F32)
    return total


def direct():
    return lax.axis_size("expert") <= 8


def share_expert(x):
    size = lax.axis_size("expert")
    if not direct():
        every = lax.all_gather(x, "expert", axis=0)
        return [every[e] for e in range(size)]
    chips = [with_expert(x, 2 * j) for j in range(size // 2)]
    return finish_expert(chips)


def finish_expert(chips):
    me = lax.axis_index("expert")
    own = jnp.stack(chips)
    other = with_expert(own, 1)
    first = me % 2 == 0
    even = jnp.where(first, own, other)
    odd = jnp.where(first, other, own)
    n = len(chips)
    even = reorder([even[j] for j in range(n)], me // 2)
    odd = reorder([odd[j] for j in range(n)], me // 2)
    return [x for pair in zip(even, odd) for x in pair]


def expert_sum_scatter(x):
    a, size, n, c = x.shape
    if not direct():
        return lax.psum_scatter(x, "expert", scatter_dimension=1, tiled=True)[:, 0]
    pairs = x.reshape(a, size // 2, 2, n, c)
    me = lax.axis_index("expert")
    first = me % 2 == 0
    mine = jnp.where(first, pairs[:, :, 0], pairs[:, :, 1])
    theirs = jnp.where(first, pairs[:, :, 1], pairs[:, :, 0]).astype(BF)
    theirs = with_expert(theirs, 1)
    half = mine + theirs.astype(F32)
    blocks = reorder([half[:, z] for z in range(size // 2)], me // 2)
    total = blocks[0]
    got = [with_expert(blocks[j].astype(BF), 2 * j) for j in range(1, size // 2)]
    for x in got:
        total = total + x.astype(F32)
    return total


class Cells:
    def __init__(self, capacity):
        size = lax.axis_size("expert")
        self.size, self.part = size, capacity + 1
        self.direct = direct()
        if self.direct:
            self.chips = size // 2
            self.cut = self.part // 8 * 8
            self.block = -(-2 * self.part // 8) * 8
            self.tail = self.block - self.cut
            self.near = self.chips * self.block
            self.total = self.near + self.chips * self.tail
            self.rows = self.near
            self.marks = (capacity, self.part + capacity)
        else:
            self.block = -(-self.part // 8) * 8
            self.total = self.rows = size * self.block
            self.marks = (capacity,)

    def index(self, routes, slot):
        if not self.direct:
            return routes * self.block + slot
        rel = routes ^ lax.axis_index("expert")
        chip, other = rel // 2, rel % 2
        near = chip * self.block + slot
        far = self.near + chip * self.tail + self.part - self.cut + slot
        return jnp.where(other == 0, near, far)

    def mark_rows(self, packed, weights):
        def write(rows, values, first, mark):
            n, height = values.shape
            values = jnp.pad(values, ((0, 0), (first, 128 - height - first)))
            hi = values.astype(BF)
            rest = values - hi.astype(F32)
            mid = rest.astype(BF)
            lo = (rest - mid.astype(F32)).astype(BF)
            line = jnp.pad(jnp.concatenate([hi, mid, lo], axis=1), ((0, 0), (0, D - 384)))
            rows = rows.reshape(n, height, D)
            at = jnp.arange(height, dtype=jnp.int32)[None, :, None] == mark
            return jnp.where(at, line[:, None, :], rows).reshape(n * height, D)

        if not self.direct:
            return [write(packed[0], weights.reshape(self.size, self.block), 0, self.marks[0])]
        near, far = weights[: self.near], weights[self.near :]
        return [
            write(packed[0], near.reshape(self.chips, self.block), 0, self.marks[0]),
            write(
                packed[1], far.reshape(self.chips, self.tail), self.cut, self.marks[1] - self.cut
            ),
        ]

    def cuts(self, packed):
        return [packed[..., : self.near], packed[..., self.near :]] if self.direct else [packed]

    def dispatch(self, packed):
        if not self.direct:
            x = packed[0].reshape(self.size, self.block, D)
            x = lax.all_to_all(x, "expert", split_axis=0, concat_axis=0, tiled=True)
            return x.reshape(self.rows, D)
        far = with_expert(packed[1], 1).reshape(self.chips, self.tail, D)
        both = packed[0].reshape(self.chips, self.block, D) + jnp.pad(
            far, ((0, 0), (self.cut, 0), (0, 0))
        )
        got = [with_expert(both[j], 2 * j) for j in range(self.chips)]
        return jnp.concatenate(got, axis=0)

    def collect(self, rows):
        if not self.direct:
            x = rows.reshape(self.size, self.block, D)
            x = lax.all_to_all(x, "expert", split_axis=0, concat_axis=0, tiled=True)
            return [x.reshape(self.total, D)]
        x = rows.reshape(self.chips, self.block, D)
        back = [with_expert(x[j], 2 * j) for j in range(self.chips)]
        far = with_expert(jnp.concatenate([y[self.cut :] for y in back], axis=0), 1)
        return [jnp.concatenate(back, axis=0), far]


def pack_quarters(attn_in, extra, me, n_dp, hw, width):
    shard = attn_in.shape[0]

    def kernel(me_ref, w_ref, extra_ref, *out_refs):
        me = me_ref[0]
        w = w_ref[...].astype(F32)
        last = extra_ref[...].astype(F32)
        for q in range(n_dp):
            cols = [w[:, g * D + q * hw : g * D + (q + 1) * hw] for g in range(3)]
            block = jnp.concatenate(cols + [last], axis=1).astype(BF)
            for k in range(n_dp):

                @pl.when((me ^ k) == q)
                def _():
                    out_refs[k][...] = block

    whole = pl.BlockSpec(memory_space=pltpu.VMEM)
    return pl.pallas_call(
        kernel,
        out_shape=[jax.ShapeDtypeStruct((shard, width), BF)] * n_dp,
        in_specs=[pl.BlockSpec(memory_space=pltpu.SMEM), whole, whole],
        out_specs=[whole] * n_dp,
        name="pack_quarters",
    )(me.reshape(1).astype(jnp.int32), attn_in, extra)


def expert_kernel(cells, w_gu, w_dn, x_list, grad_list):
    n = len(x_list)
    height = x_list[0].shape[0]
    units = w_dn.shape[0]
    widths = (D, D, 2 * units, units, D)

    def row_weights(x):
        pieces = x[:, :384].astype(F32).reshape(height // cells.block, cells.block, 384)
        row = lax.broadcasted_iota(jnp.int32, pieces.shape, 1)
        marked = row == cells.marks[0]
        for m in cells.marks[1:]:
            marked = marked | (row == m)
        line = jnp.sum(jnp.where(marked, pieces, 0.0), axis=1, keepdims=True)
        line = line[:, :, :128] + line[:, :, 128:256] + line[:, :, 256:]
        shape = (height // cells.block, cells.block, 128)
        at = lax.broadcasted_iota(jnp.int32, shape, 1) == lax.broadcasted_iota(jnp.int32, shape, 2)
        return jnp.sum(jnp.where(at, line, 0.0), axis=2, keepdims=True).reshape(height, 1)

    def kernel(gu_ref, dn_ref, *refs):
        xs, grads, outs = refs[:n], refs[n : 2 * n], refs[2 * n :]
        for i in range(n):
            produced, d_out, d_gu, hid, d_in = outs[5 * i : 5 * i + 5]
            x = xs[i][...]
            gate = mm(x, gu_ref[:, :units], ((1,), (0,)))
            up = mm(x, gu_ref[:, units:], ((1,), (0,)))
            activated, derivative = gelu_parts(gate)
            hidden = (activated * up).astype(BF)
            hid[...] = hidden
            produced[...] = mm(hidden, dn_ref[...], ((1,), (0,))).astype(BF)
            rows_in = (row_weights(x) * grads[i][...].astype(F32)).astype(BF)
            d_in[...] = rows_in
            d_hidden = mm(rows_in, dn_ref[...], ((1,), (1,)))
            d_gate = (d_hidden * up * derivative).astype(BF)
            d_up = (d_hidden * activated).astype(BF)
            d_gu[:, :units] = d_gate
            d_gu[:, units:] = d_up
            d_out[...] = (
                mm(d_gate, gu_ref[:, :units], ((1,), (1,))) + mm(d_up, gu_ref[:, units:], ((1,), (1,)))
            ).astype(BF)

    whole = pl.BlockSpec(memory_space=pltpu.VMEM)
    out = pl.pallas_call(
        kernel,
        out_shape=[jax.ShapeDtypeStruct((height, w), BF) for _ in range(n) for w in widths],
        in_specs=[whole] * (2 + 2 * n),
        out_specs=[whole] * (5 * n),
        name="expert",
    )(w_gu, w_dn, *x_list, *grad_list)
    return [list(out[j::5]) for j in range(5)]


def weight_grad(xs, ys, parts):
    m, n = xs[0].shape[1], ys[0].shape[1]
    count = len(xs)
    tile = 256
    part = n // parts

    def kernel(*refs):
        out = refs[-1]
        both = mm(refs[0][...], refs[count][...], ((0,), (0,)))
        for i in range(1, count):
            both = both + mm(refs[i][...], refs[count + i][...], ((0,), (0,)))
        if parts == 1:
            out[...] = both
        else:
            for g in range(parts):
                out[:, g, :] = both[:, g * part : (g + 1) * part]

    column = pl.BlockSpec((xs[0].shape[0], tile), lambda i: (0, i))
    whole = pl.BlockSpec(ys[0].shape, lambda i: (0, 0))
    if parts == 1:
        shape, out_spec = (m, n), pl.BlockSpec((tile, n), lambda i: (i, 0))
    else:
        shape = (m, parts, part)
        out_spec = pl.BlockSpec((tile, parts, part), lambda i: (i, 0, 0))
    return pl.pallas_call(
        kernel,
        grid=(m // tile,),
        out_shape=jax.ShapeDtypeStruct(shape, F32),
        in_specs=[column] * count + [whole] * count,
        out_specs=out_spec,
        name="weight_grad",
    )(*xs, *ys)


def on_device(
    tokens,
    cotangent,
    doc_lengths,
    routes,
    rel_bucket,
    norm1,
    attn_in,
    attn_out,
    bias_table,
    norm2,
    router,
    w_gate_up,
    w_down,
):
    rows = tokens.shape[0]
    n_dp = lax.axis_size("dp")
    n_ex = lax.axis_size("expert")
    my_dp = lax.axis_index("dp")
    capacity = max(2, TOP * rows // n_ex + 1)
    cells = Cells(capacity)
    heads = H // n_dp
    hw = heads * HD
    shard = attn_in.shape[0]

    extra = jnp.concatenate([norm1[:, None], norm2[:, None], router], axis=1)
    n_extra = extra.shape[1]
    width = -(-(3 * hw + n_extra) // 128) * 128
    extra = jnp.pad(extra, ((0, 0), (0, width - 3 * hw - n_extra)))
    sent = pack_quarters(attn_in, extra, my_dp, n_dp, hw, width)
    got = swap_dp(sent)
    w_all = share_expert(jnp.stack(reorder(got, my_dp)))
    w_pack = jnp.stack(w_all, axis=1).reshape(D, width)
    small = w_pack[:, 3 * hw : 3 * hw + n_extra].astype(F32).T
    gain_one, gain_two = small[0], small[1]
    router_all = w_pack[:, 3 * hw + 2 : 3 * hw + n_extra]
    if direct():
        out_z = jnp.stack([with_expert(attn_out.T, 2 * j) for j in range(n_ex // 2)])
        out_dp = share_dp(out_z)
        out_dp = jnp.stack(reorder(out_dp, my_dp), axis=1)
        proj_out = finish_expert([out_dp[j] for j in range(n_ex // 2)])
    else:
        proj_out = share_expert(jnp.stack(reorder(share_dp(attn_out.T), my_dp)))
    proj_out = jnp.stack(proj_out, axis=1).reshape(D, D)

    len_row = jnp.pad(doc_lengths.astype(BF), ((0, 7), (0, D - doc_lengths.shape[1])))
    group = jnp.stack(share_dp(jnp.concatenate([tokens, len_row], axis=0)))
    group_lengths = group[:, rows, : doc_lengths.shape[1]].astype(jnp.int32)
    group_in = group[:, :rows].astype(F32)

    flat_routes = routes.reshape(-1)
    route_hits = (flat_routes[:, None] == jnp.arange(n_ex, dtype=jnp.int32)[None, :]).astype(
        jnp.int32
    )
    earlier = jnp.cumsum(route_hits, axis=0) - route_hits
    slot_index = jnp.sum(earlier * route_hits, axis=1).reshape(rows, TOP)
    cell_index = cells.index(routes, slot_index)
    cell_ids = jnp.arange(cells.total, dtype=jnp.int32)
    place_bool = [cell_index[:, k][:, None] == cell_ids[None, :] for k in range(TOP)]
    place = [p.astype(BF) for p in place_bool]
    place_any = sum(place[1:], place[0])

    def packed(x):
        return [mm(p, x, ((0,), (0,))).astype(BF) for p in cells.cuts(place_any)]

    def unpacked(p, parts):
        return sum(mm(q, x, ((1,), (0,))) for q, x in zip(cells.cuts(p), parts))

    grad_out = cotangent.astype(F32)
    grad_rows = packed(cotangent)
    grad_rows = cells.dispatch(grad_rows)
    grad_rows = share_dp(grad_rows)

    inv_one = lax.rsqrt(jnp.mean(group_in * group_in, axis=-1, keepdims=True) + EPSILON)
    normed_one = (group_in * inv_one * gain_one).astype(BF).reshape(n_dp * rows, D)
    qkv = mm(normed_one, w_pack, ((1,), (0,)))[:, : 3 * hw].astype(BF)
    qkv = qkv.reshape(n_dp, rows, 3, heads, HD).transpose(2, 0, 3, 1, 4)
    queries, keys, values = qkv[0], qkv[1], qkv[2]

    doc_ends = jnp.cumsum(group_lengths, axis=1)
    places = jnp.arange(rows, dtype=jnp.int32)
    doc_index = jnp.sum(
        (places[None, :, None] >= doc_ends[:, None, :]).astype(jnp.int32), axis=2
    )
    allowed = (doc_index[:, :, None] == doc_index[:, None, :]) & (
        places[None, None, :] <= places[None, :, None]
    )
    allowed = allowed[:, None]
    distance = jnp.clip(places[:, None] - places[None, :], 0, LMAX - 1)
    dist_hot = (distance[:, :, None] == jnp.arange(LMAX, dtype=jnp.int32)[None, None, :]).astype(F32)
    bucket_hot = (rel_bucket[:, None] == jnp.arange(NB, dtype=jnp.int32)[None, :]).astype(F32)
    my_bias = lax.dynamic_slice_in_dim(bias_table, my_dp * heads, heads, axis=1)
    bias_dist = jnp.dot(bucket_hot, my_bias, precision=lax.Precision.HIGHEST)
    bias_heads = jnp.einsum("ijr,rh->hij", dist_hot, bias_dist, precision=lax.Precision.HIGHEST)

    scores = (
        jnp.einsum("phid,phjd->phij", queries, keys, preferred_element_type=F32) * SCORE_SCALE
        + bias_heads[None]
    )
    scores = jnp.where(allowed, scores, -jnp.inf)
    row_top = jnp.max(scores, axis=-1, keepdims=True)
    log_total = row_top + jnp.log(jnp.sum(jnp.exp(scores - row_top), axis=-1, keepdims=True))
    attn_probs = jnp.exp(scores - log_total)
    attn_weights = attn_probs.astype(BF)
    context_heads = jnp.einsum("phij,phjd->pihd", attn_weights, values, preferred_element_type=F32)
    context_heads = context_heads.reshape(n_dp, rows, hw).astype(BF)
    context = swap_dp([context_heads[k] for k in range(n_dp)])
    context = reorder(context, my_dp)
    context = jnp.concatenate(context, axis=1)

    inputs = tokens.astype(F32)
    residual = inputs + mm(context, proj_out, ((1,), (1,)))
    inv_two = lax.rsqrt(jnp.mean(residual * residual, axis=-1, keepdims=True) + EPSILON)
    normed_two = (residual * inv_two * gain_two).astype(BF)
    logits = mm(normed_two, router_all, ((1,), (0,)))
    route_picks = (
        routes[:, :, None] == jnp.arange(n_ex, dtype=jnp.int32)[None, None, :]
    ).astype(F32)
    chosen = jnp.sum(route_picks * logits[:, None, :], axis=2)
    chosen_exp = jnp.exp(chosen - jnp.max(chosen, axis=1, keepdims=True))
    route_weight = chosen_exp / jnp.sum(chosen_exp, axis=1, keepdims=True)

    cell_weight = sum(
        jnp.sum(jnp.where(place_bool[k], route_weight[:, k][:, None], 0.0), axis=0)
        for k in range(TOP)
    )
    arrived = cells.dispatch(cells.mark_rows(packed(normed_two), cell_weight))
    x_blocks = [with_dp(arrived, k) for k in range(n_dp - 1)]
    x_blocks.append(with_dp(arrived, n_dp - 1))

    units = w_down.shape[1]
    w_gu = w_gate_up[0].reshape(D, 2 * units)
    w_dn = w_down[0]

    first_out = expert_kernel(cells, w_gu, w_dn, x_blocks[:-1], grad_rows[:-1])
    last_out = expert_kernel(cells, w_gu, w_dn, x_blocks[-1:], grad_rows[-1:])

    def sum_back(index):
        blocks = first_out[index]
        total = blocks[0].astype(F32)
        got = [with_dp(blocks[k], k) for k in range(1, n_dp - 1)]
        got.append(with_dp(last_out[index][0], n_dp - 1))
        for x in got:
            total = total + x.astype(F32)
        return total.astype(BF)

    returned = cells.collect(sum_back(0))
    d_returned = cells.collect(sum_back(1))
    d_gate_up, hidden, d_rows_in = (first_out[i] + last_out[i] for i in (2, 3, 4))
    d_w_gate_up = weight_grad(x_blocks, d_gate_up, 2)[None]
    d_w_down = weight_grad(hidden, d_rows_in, 1)[None]

    expert_out = [unpacked(p, returned) for p in place]
    output = (
        residual + sum(route_weight[:, k][:, None] * expert_out[k] for k in range(TOP))
    ).astype(BF)
    d_route_weight = jnp.stack([jnp.sum(grad_out * e, axis=1) for e in expert_out], axis=1)
    route_delta = d_route_weight - jnp.sum(d_route_weight * route_weight, axis=1, keepdims=True)
    d_logits = jnp.sum(route_picks * (route_weight * route_delta)[:, :, None], axis=1).astype(BF)
    d_router_part = mm(normed_two, d_logits, ((0,), (0,)))
    d_normed_two = unpacked(place_any, d_returned) + mm(d_logits, router_all, ((1,), (1,)))
    scaled = gain_two * d_normed_two
    d_norm2_part = jnp.sum(d_normed_two * residual * inv_two, axis=0)
    d_residual = (
        grad_out
        + inv_two * scaled
        - residual
        * (inv_two * inv_two * inv_two)
        * jnp.mean(scaled * residual, axis=-1, keepdims=True)
    )
    d_residual_b = d_residual.astype(BF)
    d_context = mm(d_residual_b, proj_out, ((1,), (0,))).astype(BF)
    d_ctx = reorder([d_context[:, q * hw : (q + 1) * hw] for q in range(n_dp)], my_dp)
    d_heads = jnp.stack(swap_dp(d_ctx)).reshape(n_dp, rows, heads, HD)
    d_out_part = mm(d_residual_b, context, ((0,), (0,)))
    d_out_rows = expert_sum_scatter(d_out_part.reshape(n_dp, n_ex, shard, D)).astype(BF)

    d_probs = jnp.einsum("pihd,phjd->phij", d_heads, values, preferred_element_type=F32)
    row_delta = jnp.sum(attn_probs * d_probs, axis=-1, keepdims=True)
    d_scores = jnp.where(allowed, attn_probs * (d_probs - row_delta), 0.0)
    d_scores_b = d_scores.astype(BF)
    d_queries = (
        jnp.einsum("phij,phjd->pihd", d_scores_b, keys, preferred_element_type=F32) * SCORE_SCALE
    ).astype(BF)
    d_keys = (
        jnp.einsum("phij,phid->pjhd", d_scores_b, queries, preferred_element_type=F32)
        * SCORE_SCALE
    ).astype(BF)
    d_values = jnp.einsum(
        "phij,pihd->pjhd", attn_weights, d_heads, preferred_element_type=F32
    ).astype(BF)
    d_qkv = jnp.concatenate(
        [g.reshape(n_dp * rows, hw) for g in (d_queries, d_keys, d_values)]
        + [jnp.zeros((n_dp * rows, width - 3 * hw), BF)],
        axis=1,
    )
    d_normed_part = mm(d_qkv, w_pack, ((1,), (1,))).reshape(n_dp, rows, D)
    d_norm1_part = jnp.sum(d_normed_part * group_in * inv_one, axis=(0, 1))
    d_in_part = mm(normed_one, d_qkv, ((0,), (0,)))
    extra_part = jnp.concatenate(
        [jnp.stack([d_norm1_part, d_norm2_part], axis=1), d_router_part], axis=1
    )
    extra_part = jnp.pad(extra_part, ((0, 0), (3 * hw, width - 3 * hw - n_extra)))
    d_pack = d_in_part + extra_part
    d_pack_rows = expert_sum_scatter(d_pack.reshape(n_dp, n_ex, shard, width)).astype(BF)

    d_dist = jnp.einsum(
        "hij,ijr->hr", jnp.sum(d_scores, axis=0), dist_hot, precision=lax.Precision.HIGHEST
    )
    d_bias = jnp.dot(d_dist, bucket_hot, precision=lax.Precision.HIGHEST)
    d_bias = jnp.pad(d_bias.reshape(1, heads * NB), ((0, 0), (0, 128 - heads * NB)))
    step = 1
    while step < n_ex:
        d_bias = d_bias + with_expert(d_bias, step)
        step *= 2
    bias_hi = d_bias.astype(BF)
    bias_lo = (d_bias - bias_hi.astype(F32)).astype(BF)
    bias_row = jnp.pad(jnp.concatenate([bias_hi, bias_lo], axis=1), ((0, 0), (0, width + D - 256)))

    last = jnp.concatenate([d_pack_rows, d_out_rows], axis=2)
    last = [
        jnp.concatenate([x, bias_row], axis=0)
        for x in reorder([last[q] for q in range(n_dp)], my_dp)
    ]
    last = swap_dp(last)
    last = jnp.stack(reorder(last, my_dp)).astype(F32)
    d_attn_in = (
        last[:, :shard, : 3 * hw].reshape(n_dp, shard, 3, hw).transpose(1, 2, 0, 3)
    ).reshape(shard, 3 * n_dp * hw)
    d_extra = jnp.sum(last[:, :shard, 3 * hw : 3 * hw + n_extra], axis=0)
    d_norm1, d_norm2, d_router = d_extra[:, 0], d_extra[:, 1], d_extra[:, 2:]
    d_attn_out = jnp.sum(last[:, :shard, width:], axis=0).T
    d_bias = last[:, shard, :128] + last[:, shard, 128:256]
    d_bias_table = d_bias[:, : heads * NB].reshape(H, NB).T

    d_normed_b = d_normed_part.astype(BF)
    d_normed_one = sum_dp([d_normed_b[k] for k in range(n_dp)])
    inv_mine = inv_one[0]
    scaled_one = gain_one * d_normed_one
    d_tokens = (
        d_residual
        + inv_mine * scaled_one
        - inputs
        * (inv_mine * inv_mine * inv_mine)
        * jnp.mean(scaled_one * inputs, axis=-1, keepdims=True)
    )

    return (
        output,
        d_tokens,
        d_norm1,
        d_attn_in,
        d_attn_out,
        d_bias_table,
        d_norm2,
        d_router,
        d_w_gate_up,
        d_w_down,
    )


def solution(mesh):
    both = ("dp", "expert")
    in_specs = (
        P(both, None),
        P(both, None),
        P(both, None),
        P(both, None),
        P(),
        P(both),
        P(both, None),
        P(None, both),
        P(),
        P(both),
        P(both, None),
        P("expert", None, None, "dp"),
        P("expert", "dp", None),
    )
    out_specs = (
        P(both, None),
        P(both, None),
        P(both),
        P(both, None),
        P(None, both),
        P(),
        P(both),
        P(both, None),
        P("expert", None, None, "dp"),
        P("expert", "dp", None),
    )

    return jax.shard_map(
        on_device, mesh=mesh, in_specs=in_specs, out_specs=out_specs, check_vma=False
    )
```

```python
import jax
import jax.numpy as jnp
from jax import lax
from jax.experimental import pallas as pl
from jax.experimental.pallas import tpu as pltpu
from jax.sharding import PartitionSpec as P

D = 768
H = 12
HD = 64
TOP = 2
NB = 32
LMAX = 96

EPSILON = 1e-06
GELU_COEF = 0.7978845608028654
GELU_CUBE = 0.044715
SCORE_SCALE = 0.125

BF = jnp.bfloat16
F32 = jnp.float32


def gelu_parts(gate_in):
    inner_arg = GELU_COEF * (gate_in + GELU_CUBE * gate_in * gate_in * gate_in)
    tanh_part = jnp.tanh(inner_arg)
    result = 0.5 * gate_in * (1.0 + tanh_part)
    derivative = 0.5 * (1.0 + tanh_part) + 0.5 * gate_in * (
        1.0 - tanh_part * tanh_part
    ) * GELU_COEF * (1.0 + 3.0 * GELU_CUBE * gate_in * gate_in)
    return (result, derivative)


def mm(a, b, dims):
    return lax.dot_general(a, b, (dims, ((), ())), preferred_element_type=F32)


def reorder(blocks, me):
    bit = 1
    while bit < len(blocks):
        on = (me & bit) != 0
        blocks = [jnp.where(on, blocks[q ^ bit], blocks[q]) for q in range(len(blocks))]
        bit *= 2
    return blocks


def with_dp(x, k):
    size = lax.axis_size("dp")
    return lax.ppermute(x, "dp", [(i, i ^ k) for i in range(size)]) if k else x


def with_expert(x, k):
    size = lax.axis_size("expert")
    return lax.ppermute(x, "expert", [(i, i ^ k) for i in range(size)]) if k else x


def n_dp_of():
    return lax.axis_size("dp")


def share_dp(x):
    return [with_dp(x, k) for k in range(n_dp_of())]


def swap_dp(blocks):
    return [with_dp(x, k) for k, x in enumerate(blocks)]


def sum_dp(blocks):
    total = blocks[0].astype(F32)
    for k in range(1, len(blocks)):
        total = total + with_dp(blocks[k], k).astype(F32)
    return total


def direct():
    return lax.axis_size("expert") <= 8


def share_expert(x):
    size = lax.axis_size("expert")
    if not direct():
        every = lax.all_gather(x, "expert", axis=0)
        return [every[e] for e in range(size)]
    chips = [with_expert(x, 2 * j) for j in range(size // 2)]
    return finish_expert(chips)


def finish_expert(chips):
    me = lax.axis_index("expert")
    own = jnp.stack(chips)
    other = with_expert(own, 1)
    first = me % 2 == 0
    even = jnp.where(first, own, other)
    odd = jnp.where(first, other, own)
    n = len(chips)
    even = reorder([even[j] for j in range(n)], me // 2)
    odd = reorder([odd[j] for j in range(n)], me // 2)
    return [x for pair in zip(even, odd) for x in pair]


def expert_sum_scatter(x):
    a, size, n, c = x.shape
    if not direct():
        return lax.psum_scatter(x, "expert", scatter_dimension=1, tiled=True)[:, 0]
    pairs = x.reshape(a, size // 2, 2, n, c)
    me = lax.axis_index("expert")
    first = me % 2 == 0
    mine = jnp.where(first, pairs[:, :, 0], pairs[:, :, 1])
    theirs = jnp.where(first, pairs[:, :, 1], pairs[:, :, 0]).astype(BF)
    theirs = with_expert(theirs, 1)
    half = mine + theirs.astype(F32)
    blocks = reorder([half[:, z] for z in range(size // 2)], me // 2)
    total = blocks[0]
    got = [with_expert(blocks[j].astype(BF), 2 * j) for j in range(1, size // 2)]
    for x in got:
        total = total + x.astype(F32)
    return total


class Cells:
    def __init__(self, capacity):
        size = lax.axis_size("expert")
        self.size, self.part = size, capacity + 1
        self.direct = direct()
        if self.direct:
            self.chips = size // 2
            self.cut = self.part // 8 * 8
            self.block = -(-2 * self.part // 8) * 8
            self.tail = self.block - self.cut
            self.near = self.chips * self.block
            self.total = self.near + self.chips * self.tail
            self.rows = self.near
            self.marks = (capacity, self.part + capacity)
        else:
            self.block = -(-self.part // 8) * 8
            self.total = self.rows = size * self.block
            self.marks = (capacity,)

    def index(self, routes, slot):
        if not self.direct:
            return routes * self.block + slot
        rel = routes ^ lax.axis_index("expert")
        chip, other = rel // 2, rel % 2
        near = chip * self.block + slot
        far = self.near + chip * self.tail + self.part - self.cut + slot
        return jnp.where(other == 0, near, far)

    def mark_rows(self, packed, weights):
        def write(rows, values, first, mark):
            n, height = values.shape
            values = jnp.pad(values, ((0, 0), (first, 128 - height - first)))
            hi = values.astype(BF)
            rest = values - hi.astype(F32)
            mid = rest.astype(BF)
            lo = (rest - mid.astype(F32)).astype(BF)
            line = jnp.pad(jnp.concatenate([hi, mid, lo], axis=1), ((0, 0), (0, D - 384)))
            rows = rows.reshape(n, height, D)
            at = jnp.arange(height, dtype=jnp.int32)[None, :, None] == mark
            return jnp.where(at, line[:, None, :], rows).reshape(n * height, D)

        if not self.direct:
            return [write(packed[0], weights.reshape(self.size, self.block), 0, self.marks[0])]
        near, far = weights[: self.near], weights[self.near :]
        return [
            write(packed[0], near.reshape(self.chips, self.block), 0, self.marks[0]),
            write(
                packed[1], far.reshape(self.chips, self.tail), self.cut, self.marks[1] - self.cut
            ),
        ]

    def cuts(self, packed):
        return [packed[..., : self.near], packed[..., self.near :]] if self.direct else [packed]

    def dispatch(self, packed):
        if not self.direct:
            x = packed[0].reshape(self.size, self.block, D)
            x = lax.all_to_all(x, "expert", split_axis=0, concat_axis=0, tiled=True)
            return x.reshape(self.rows, D)
        far = with_expert(packed[1], 1).reshape(self.chips, self.tail, D)
        both = packed[0].reshape(self.chips, self.block, D) + jnp.pad(
            far, ((0, 0), (self.cut, 0), (0, 0))
        )
        got = [with_expert(both[j], 2 * j) for j in range(self.chips)]
        return jnp.concatenate(got, axis=0)

    def collect(self, rows):
        if not self.direct:
            x = rows.reshape(self.size, self.block, D)
            x = lax.all_to_all(x, "expert", split_axis=0, concat_axis=0, tiled=True)
            return [x.reshape(self.total, D)]
        x = rows.reshape(self.chips, self.block, D)
        back = [with_expert(x[j], 2 * j) for j in range(self.chips)]
        far = with_expert(jnp.concatenate([y[self.cut :] for y in back], axis=0), 1)
        return [jnp.concatenate(back, axis=0), far]


def pack_quarters(attn_in, norm1, norm2, router, me, n_dp, hw, width):
    shard = attn_in.shape[0]
    spare = width - 3 * hw - 2 - router.shape[1]

    def column(row):
        shape = (shard, shard)
        at = lax.broadcasted_iota(jnp.int32, shape, 0) == lax.broadcasted_iota(jnp.int32, shape, 1)
        return jnp.sum(jnp.where(at, row.astype(F32), 0.0), axis=1, keepdims=True)

    def kernel(me_ref, w_ref, one_ref, two_ref, router_ref, *out_refs):
        me = me_ref[0]
        w = w_ref[...].astype(F32)
        last = [
            column(one_ref[...]),
            column(two_ref[...]),
            router_ref[...].astype(F32),
            jnp.zeros((shard, spare), F32),
        ]
        for q in range(n_dp):
            cols = [w[:, g * D + q * hw : g * D + (q + 1) * hw] for g in range(3)]
            block = jnp.concatenate(cols + last, axis=1).astype(BF)
            for k in range(n_dp):

                @pl.when((me ^ k) == q)
                def _():
                    out_refs[k][...] = block

    whole = pl.BlockSpec(memory_space=pltpu.VMEM)
    return pl.pallas_call(
        kernel,
        out_shape=[jax.ShapeDtypeStruct((shard, width), BF)] * n_dp,
        in_specs=[pl.BlockSpec(memory_space=pltpu.SMEM)] + [whole] * 4,
        out_specs=[whole] * n_dp,
        name="pack",
    )(me.reshape(1).astype(jnp.int32), attn_in, norm1, norm2, router)


def expert_kernel(cells, w_gu, w_dn, x_list, grad_list):
    n = len(x_list)
    height = x_list[0].shape[0]
    units = w_dn.shape[0]
    widths = (D, D, 2 * units, units, D)

    def row_weights(x):
        pieces = x[:, :384].astype(F32).reshape(height // cells.block, cells.block, 384)
        row = lax.broadcasted_iota(jnp.int32, pieces.shape, 1)
        marked = row == cells.marks[0]
        for m in cells.marks[1:]:
            marked = marked | (row == m)
        line = jnp.sum(jnp.where(marked, pieces, 0.0), axis=1, keepdims=True)
        line = line[:, :, :128] + line[:, :, 128:256] + line[:, :, 256:]
        shape = (height // cells.block, cells.block, 128)
        at = lax.broadcasted_iota(jnp.int32, shape, 1) == lax.broadcasted_iota(jnp.int32, shape, 2)
        return jnp.sum(jnp.where(at, line, 0.0), axis=2, keepdims=True).reshape(height, 1)

    def kernel(gu_ref, dn_ref, *refs):
        xs, grads, outs = refs[:n], refs[n : 2 * n], refs[2 * n :]
        for i in range(n):
            produced, d_out, d_gu, hid, d_in = outs[5 * i : 5 * i + 5]
            x = xs[i][...]
            gate = mm(x, gu_ref[:, :units], ((1,), (0,)))
            up = mm(x, gu_ref[:, units:], ((1,), (0,)))
            activated, derivative = gelu_parts(gate)
            hidden = (activated * up).astype(BF)
            hid[...] = hidden
            produced[...] = mm(hidden, dn_ref[...], ((1,), (0,))).astype(BF)
            rows_in = (row_weights(x) * grads[i][...].astype(F32)).astype(BF)
            d_in[...] = rows_in
            d_hidden = mm(rows_in, dn_ref[...], ((1,), (1,)))
            d_gate = (d_hidden * up * derivative).astype(BF)
            d_up = (d_hidden * activated).astype(BF)
            d_gu[:, :units] = d_gate
            d_gu[:, units:] = d_up
            d_out[...] = (
                mm(d_gate, gu_ref[:, :units], ((1,), (1,))) + mm(d_up, gu_ref[:, units:], ((1,), (1,)))
            ).astype(BF)

    whole = pl.BlockSpec(memory_space=pltpu.VMEM)
    out = pl.pallas_call(
        kernel,
        out_shape=[jax.ShapeDtypeStruct((height, w), BF) for _ in range(n) for w in widths],
        in_specs=[whole] * (2 + 2 * n),
        out_specs=[whole] * (5 * n),
        name="expert",
    )(w_gu, w_dn, *x_list, *grad_list)
    return [list(out[j::5]) for j in range(5)]


def weight_grad(xs, ys, parts):
    m, n = xs[0].shape[1], ys[0].shape[1]
    count = len(xs)
    tile = 256
    part = n // parts

    def kernel(*refs):
        out = refs[-1]
        both = mm(refs[0][...], refs[count][...], ((0,), (0,)))
        for i in range(1, count):
            both = both + mm(refs[i][...], refs[count + i][...], ((0,), (0,)))
        if parts == 1:
            out[...] = both
        else:
            for g in range(parts):
                out[:, g, :] = both[:, g * part : (g + 1) * part]

    column = pl.BlockSpec((xs[0].shape[0], tile), lambda i: (0, i))
    whole = pl.BlockSpec(ys[0].shape, lambda i: (0, 0))
    if parts == 1:
        shape, out_spec = (m, n), pl.BlockSpec((tile, n), lambda i: (i, 0))
    else:
        shape = (m, parts, part)
        out_spec = pl.BlockSpec((tile, parts, part), lambda i: (i, 0, 0))
    return pl.pallas_call(
        kernel,
        grid=(m // tile,),
        out_shape=jax.ShapeDtypeStruct(shape, F32),
        in_specs=[column] * count + [whole] * count,
        out_specs=out_spec,
        name="wg",
    )(*xs, *ys)


def on_device(
    tokens,
    cotangent,
    doc_lengths,
    routes,
    rel_bucket,
    norm1,
    attn_in,
    attn_out,
    bias_table,
    norm2,
    router,
    w_gate_up,
    w_down,
):
    rows = tokens.shape[0]
    n_dp = lax.axis_size("dp")
    n_ex = lax.axis_size("expert")
    my_dp = lax.axis_index("dp")
    capacity = max(2, TOP * rows // n_ex + 1)
    cells = Cells(capacity)
    heads = H // n_dp
    hw = heads * HD
    shard = attn_in.shape[0]

    n_extra = 2 + router.shape[1]
    width = -(-(3 * hw + n_extra) // 128) * 128
    sent = pack_quarters(attn_in, norm1[None], norm2[None], router, my_dp, n_dp, hw, width)
    got = swap_dp(sent)
    w_all = share_expert(jnp.stack(reorder(got, my_dp)))
    w_pack = jnp.stack(w_all, axis=1).reshape(D, width)
    small = w_pack[:, 3 * hw : 3 * hw + n_extra].astype(F32).T
    gain_one, gain_two = small[0], small[1]
    router_all = w_pack[:, 3 * hw + 2 : 3 * hw + n_extra]
    if direct():
        out_z = jnp.stack([with_expert(attn_out.T, 2 * j) for j in range(n_ex // 2)])
        out_dp = share_dp(out_z)
        out_dp = jnp.stack(reorder(out_dp, my_dp), axis=1)
        proj_out = finish_expert([out_dp[j] for j in range(n_ex // 2)])
    else:
        proj_out = share_expert(jnp.stack(reorder(share_dp(attn_out.T), my_dp)))
    proj_out = jnp.stack(proj_out, axis=1).reshape(D, D)

    len_row = jnp.pad(doc_lengths.astype(BF), ((0, 7), (0, D - doc_lengths.shape[1])))
    group = jnp.stack(share_dp(jnp.concatenate([tokens, len_row], axis=0)))
    group_lengths = group[:, rows, : doc_lengths.shape[1]].astype(jnp.int32)
    group_in = group[:, :rows].astype(F32)

    flat_routes = routes.reshape(-1)
    route_hits = (flat_routes[:, None] == jnp.arange(n_ex, dtype=jnp.int32)[None, :]).astype(
        jnp.int32
    )
    earlier = jnp.cumsum(route_hits, axis=0) - route_hits
    slot_index = jnp.sum(earlier * route_hits, axis=1).reshape(rows, TOP)
    cell_index = cells.index(routes, slot_index)
    cell_ids = jnp.arange(cells.total, dtype=jnp.int32)
    place_bool = [cell_index[:, k][:, None] == cell_ids[None, :] for k in range(TOP)]
    place = [p.astype(BF) for p in place_bool]
    place_any = sum(place[1:], place[0])

    def packed(x):
        return [mm(p, x, ((0,), (0,))).astype(BF) for p in cells.cuts(place_any)]

    def unpacked(p, parts):
        return sum(mm(q, x, ((1,), (0,))) for q, x in zip(cells.cuts(p), parts))

    grad_out = cotangent.astype(F32)
    grad_rows = packed(cotangent)
    grad_rows = cells.dispatch(grad_rows)
    grad_rows = share_dp(grad_rows)

    inv_one = lax.rsqrt(jnp.mean(group_in * group_in, axis=-1, keepdims=True) + EPSILON)
    normed_one = (group_in * inv_one * gain_one).astype(BF).reshape(n_dp * rows, D)
    qkv = mm(normed_one, w_pack, ((1,), (0,)))[:, : 3 * hw].astype(BF)
    qkv = qkv.reshape(n_dp, rows, 3, heads, HD).transpose(2, 0, 3, 1, 4)
    queries, keys, values = qkv[0], qkv[1], qkv[2]

    doc_ends = jnp.cumsum(group_lengths, axis=1)
    places = jnp.arange(rows, dtype=jnp.int32)
    doc_index = jnp.sum(
        (places[None, :, None] >= doc_ends[:, None, :]).astype(jnp.int32), axis=2
    )
    allowed = (doc_index[:, :, None] == doc_index[:, None, :]) & (
        places[None, None, :] <= places[None, :, None]
    )
    allowed = allowed[:, None]
    distance = jnp.clip(places[:, None] - places[None, :], 0, LMAX - 1)
    dist_hot = (distance[:, :, None] == jnp.arange(LMAX, dtype=jnp.int32)[None, None, :]).astype(F32)
    bucket_hot = (rel_bucket[:, None] == jnp.arange(NB, dtype=jnp.int32)[None, :]).astype(F32)
    my_bias = lax.dynamic_slice_in_dim(bias_table, my_dp * heads, heads, axis=1)
    bias_dist = jnp.dot(bucket_hot, my_bias, precision=lax.Precision.HIGHEST)
    bias_heads = jnp.einsum("ijr,rh->hij", dist_hot, bias_dist, precision=lax.Precision.HIGHEST)

    scores = (
        jnp.einsum("phid,phjd->phij", queries, keys, preferred_element_type=F32) * SCORE_SCALE
        + bias_heads[None]
    )
    scores = jnp.where(allowed, scores, -jnp.inf)
    row_top = jnp.max(scores, axis=-1, keepdims=True)
    log_total = row_top + jnp.log(jnp.sum(jnp.exp(scores - row_top), axis=-1, keepdims=True))
    attn_probs = jnp.exp(scores - log_total)
    attn_weights = attn_probs.astype(BF)
    context_heads = jnp.einsum("phij,phjd->pihd", attn_weights, values, preferred_element_type=F32)
    context_heads = context_heads.reshape(n_dp, rows, hw).astype(BF)
    context = swap_dp([context_heads[k] for k in range(n_dp)])
    context = reorder(context, my_dp)
    context = jnp.concatenate(context, axis=1)

    inputs = tokens.astype(F32)
    residual = inputs + mm(context, proj_out, ((1,), (1,)))
    inv_two = lax.rsqrt(jnp.mean(residual * residual, axis=-1, keepdims=True) + EPSILON)
    normed_two = (residual * inv_two * gain_two).astype(BF)
    logits = mm(normed_two, router_all, ((1,), (0,)))
    route_picks = (
        routes[:, :, None] == jnp.arange(n_ex, dtype=jnp.int32)[None, None, :]
    ).astype(F32)
    chosen = jnp.sum(route_picks * logits[:, None, :], axis=2)
    chosen_exp = jnp.exp(chosen - jnp.max(chosen, axis=1, keepdims=True))
    route_weight = chosen_exp / jnp.sum(chosen_exp, axis=1, keepdims=True)

    cell_weight = sum(
        jnp.sum(jnp.where(place_bool[k], route_weight[:, k][:, None], 0.0), axis=0)
        for k in range(TOP)
    )
    arrived = cells.dispatch(cells.mark_rows(packed(normed_two), cell_weight))
    units = w_down.shape[1]
    arrived, w_gu = lax.optimization_barrier((arrived, w_gate_up[0].reshape(D, 2 * units)))
    x_blocks = [with_dp(arrived, k) for k in range(n_dp - 1)]
    x_blocks.append(with_dp(arrived, n_dp - 1))

    w_dn = w_down[0]

    first_out = expert_kernel(cells, w_gu, w_dn, x_blocks[:-1], grad_rows[:-1])
    last_out = expert_kernel(cells, w_gu, w_dn, x_blocks[-1:], grad_rows[-1:])

    def sum_back(index):
        blocks = first_out[index]
        total = blocks[0].astype(F32)
        got = [with_dp(blocks[k], k) for k in range(1, n_dp - 1)]
        got.append(with_dp(last_out[index][0], n_dp - 1))
        for x in got:
            total = total + x.astype(F32)
        return total.astype(BF)

    returned = cells.collect(sum_back(0))
    d_returned = cells.collect(sum_back(1))
    d_gate_up, hidden, d_rows_in = (first_out[i] + last_out[i] for i in (2, 3, 4))
    d_w_gate_up = weight_grad(x_blocks, d_gate_up, 2)[None]
    d_w_down = weight_grad(hidden, d_rows_in, 1)[None]

    expert_out = [unpacked(p, returned) for p in place]
    output = (
        residual + sum(route_weight[:, k][:, None] * expert_out[k] for k in range(TOP))
    ).astype(BF)
    d_route_weight = jnp.stack([jnp.sum(grad_out * e, axis=1) for e in expert_out], axis=1)
    route_delta = d_route_weight - jnp.sum(d_route_weight * route_weight, axis=1, keepdims=True)
    d_logits = jnp.sum(route_picks * (route_weight * route_delta)[:, :, None], axis=1).astype(BF)
    d_router_part = mm(normed_two, d_logits, ((0,), (0,)))
    d_normed_two = unpacked(place_any, d_returned) + mm(d_logits, router_all, ((1,), (1,)))
    scaled = gain_two * d_normed_two
    d_norm2_part = jnp.sum(d_normed_two * residual * inv_two, axis=0)
    d_residual = (
        grad_out
        + inv_two * scaled
        - residual
        * (inv_two * inv_two * inv_two)
        * jnp.mean(scaled * residual, axis=-1, keepdims=True)
    )
    d_residual_b = d_residual.astype(BF)
    d_context = mm(d_residual_b, proj_out, ((1,), (0,))).astype(BF)
    d_ctx = reorder([d_context[:, q * hw : (q + 1) * hw] for q in range(n_dp)], my_dp)
    d_heads = jnp.stack(swap_dp(d_ctx)).reshape(n_dp, rows, heads, HD)
    d_out_part = mm(d_residual_b, context, ((0,), (0,)))
    d_out_rows = expert_sum_scatter(d_out_part.reshape(n_dp, n_ex, shard, D)).astype(BF)

    d_probs = jnp.einsum("pihd,phjd->phij", d_heads, values, preferred_element_type=F32)
    row_delta = jnp.sum(attn_probs * d_probs, axis=-1, keepdims=True)
    d_scores = jnp.where(allowed, attn_probs * (d_probs - row_delta), 0.0)
    d_scores_b = d_scores.astype(BF)
    d_queries = (
        jnp.einsum("phij,phjd->pihd", d_scores_b, keys, preferred_element_type=F32) * SCORE_SCALE
    ).astype(BF)
    d_keys = (
        jnp.einsum("phij,phid->pjhd", d_scores_b, queries, preferred_element_type=F32)
        * SCORE_SCALE
    ).astype(BF)
    d_values = jnp.einsum(
        "phij,pihd->pjhd", attn_weights, d_heads, preferred_element_type=F32
    ).astype(BF)
    d_qkv = jnp.concatenate(
        [g.reshape(n_dp * rows, hw) for g in (d_queries, d_keys, d_values)]
        + [jnp.zeros((n_dp * rows, width - 3 * hw), BF)],
        axis=1,
    )
    d_normed_part = mm(d_qkv, w_pack, ((1,), (1,))).reshape(n_dp, rows, D)
    d_norm1_part = jnp.sum(d_normed_part * group_in * inv_one, axis=(0, 1))
    d_in_part = mm(normed_one, d_qkv, ((0,), (0,)))
    extra_part = jnp.concatenate(
        [jnp.stack([d_norm1_part, d_norm2_part], axis=1), d_router_part], axis=1
    )
    extra_part = jnp.pad(extra_part, ((0, 0), (3 * hw, width - 3 * hw - n_extra)))
    d_pack = d_in_part + extra_part
    d_pack_rows = expert_sum_scatter(d_pack.reshape(n_dp, n_ex, shard, width)).astype(BF)

    d_dist = jnp.einsum(
        "hij,ijr->hr", jnp.sum(d_scores, axis=0), dist_hot, precision=lax.Precision.HIGHEST
    )
    d_bias = jnp.dot(d_dist, bucket_hot, precision=lax.Precision.HIGHEST)
    d_bias = jnp.pad(d_bias.reshape(1, heads * NB), ((0, 0), (0, 128 - heads * NB)))
    step = 1
    while step < n_ex:
        d_bias = d_bias + with_expert(d_bias, step)
        step *= 2
    bias_hi = d_bias.astype(BF)
    bias_lo = (d_bias - bias_hi.astype(F32)).astype(BF)
    bias_row = jnp.pad(jnp.concatenate([bias_hi, bias_lo], axis=1), ((0, 0), (0, width + D - 256)))

    last = jnp.concatenate([d_pack_rows, d_out_rows], axis=2)
    last = [
        jnp.concatenate([x, bias_row], axis=0)
        for x in reorder([last[q] for q in range(n_dp)], my_dp)
    ]
    last = swap_dp(last)
    last = jnp.stack(reorder(last, my_dp)).astype(F32)
    d_attn_in = (
        last[:, :shard, : 3 * hw].reshape(n_dp, shard, 3, hw).transpose(1, 2, 0, 3)
    ).reshape(shard, 3 * n_dp * hw)
    d_extra = jnp.sum(last[:, :shard, 3 * hw : 3 * hw + n_extra], axis=0)
    d_norm1, d_norm2, d_router = d_extra[:, 0], d_extra[:, 1], d_extra[:, 2:]
    d_attn_out = jnp.sum(last[:, :shard, width:], axis=0).T
    d_bias = last[:, shard, :128] + last[:, shard, 128:256]
    d_bias_table = d_bias[:, : heads * NB].reshape(H, NB).T

    d_normed_b = d_normed_part.astype(BF)
    d_normed_one = sum_dp([d_normed_b[k] for k in range(n_dp)])
    inv_mine = inv_one[0]
    scaled_one = gain_one * d_normed_one
    d_tokens = (
        d_residual
        + inv_mine * scaled_one
        - inputs
        * (inv_mine * inv_mine * inv_mine)
        * jnp.mean(scaled_one * inputs, axis=-1, keepdims=True)
    )

    return (
        output,
        d_tokens,
        d_norm1,
        d_attn_in,
        d_attn_out,
        d_bias_table,
        d_norm2,
        d_router,
        d_w_gate_up,
        d_w_down,
    )


def solution(mesh):
    both = ("dp", "expert")
    in_specs = (
        P(both, None),
        P(both, None),
        P(both, None),
        P(both, None),
        P(),
        P(both),
        P(both, None),
        P(None, both),
        P(),
        P(both),
        P(both, None),
        P("expert", None, None, "dp"),
        P("expert", "dp", None),
    )
    out_specs = (
        P(both, None),
        P(both, None),
        P(both),
        P(both, None),
        P(None, both),
        P(),
        P(both),
        P(both, None),
        P("expert", None, None, "dp"),
        P("expert", "dp", None),
    )

    return jax.shard_map(
        on_device, mesh=mesh, in_specs=in_specs, out_specs=out_specs, check_vma=False
    )
```
